256 devices in a mesh: queue: 16 (over z_hi, y, core), seq: 16 (over z_lo, x).
Axes of the slice: x: 4, y: 4, z: 8 (z_hi: 2, z_lo: 4; z = z_hi * 4 + z_lo), core: 2. Of those that a mesh axis runs over, the one named last changes fastest.
Arguments:
- latents: float32 [64, 16, 2048], P('queue', None, 'seq'), may hold values from -6 to 6
- step_index: int32 [64], P('queue'), may hold values from 0 to 29, as said below
- levels: float32 [31], replicated, may hold values from 0 to 1, as said below
- modulation: float32 [30, 5, 1152], replicated, may hold values from -4 to 4
- embed_weight: bfloat16 [16, 1152], replicated, may hold values from -1.5 to 1.5
- position: bfloat16 [2048, 1152], P('seq'), may hold values from -3 to 3
- qkv_weight: bfloat16 [1152, 3456], replicated, may hold values from -0.1875 to 0.1875
- q_gain: float32 [72], replicated, may hold values from 1 to 2.5
- k_gain: float32 [72], replicated, may hold values from 1 to 2.5
- text_kv: bfloat16 [2, 128, 1152], P(None, None, 'seq'), may hold values from -6 to 6
- out_weight: bfloat16 [1152, 1152], replicated, may hold values from -0.1875 to 0.1875
- final_weight: bfloat16 [1152, 16], replicated, may hold values from -0.1875 to 0.1875
- new_noise: float32 [16, 2048], P(None, 'seq'), may hold values from -6 to 6
Outputs:
- advanced: float32 [64, 16, 2048], P('queue', None, 'seq')
- velocity: float32 [64, 16, 2048], P('queue', None, 'seq')
The draws below stay inside these ranges and needn't reach their ends.
Inputs may be any that keep to these rules, and one draw needn't show every extreme that they name: `step_index`: frame 0 has index 0 and the last frame 30 - 1; frame j otherwise has j * 30 // 64 or one more, at most 29. levels rise strictly from exactly 0 at index 0 to exactly 1 at index 30.
All inputs are finite; a program needn't handle non-finite values.
Results may differ from the reference program's by a relative error of at most 0.0044.
Values may be sent and summed in bfloat16 or wider, within the bound.
A program may use at most 128 MiB of HBM per device.

```python
import math
import jax
import jax.numpy as jnp
from jax import lax

D = 1152
HEADS = 16
HD = 72
C = 16
TXT = 128
STEPS = 30
FRAMES = 64
TOKENS = 2048


def draw_step_index(key, part):
    places = jnp.arange(FRAMES, dtype=jnp.int32)
    base_index = places * STEPS // FRAMES
    jitter = jax.random.randint(key, (FRAMES,), 0, 2, dtype=jnp.int32)
    chosen = jnp.clip(base_index + jitter, 0, STEPS - 1)
    chosen = jnp.where(places == 0, 0, chosen)
    chosen = jnp.where(places == FRAMES - 1, STEPS - 1, chosen)
    return chosen.astype(jnp.int32)


def draw_levels(key, part):
    increments = jax.random.uniform(key, (STEPS,), jnp.float32, 0.3, 1.7)
    rising = jnp.concatenate([jnp.zeros((1,), jnp.float32), jnp.cumsum(increments)]) / jnp.sum(increments)
    places = jnp.arange(STEPS + 1)
    return jnp.where(places == STEPS, 1.0, rising).astype(jnp.float32)


def block_levels(own_key, dims, pieces, least, top_value):
    def one(dim, parts):
        steps = jax.random.uniform(jax.random.fold_in(jax.random.fold_in(own_key, 6), dim), (parts,), jnp.float32, least / len(pieces), top_value / len(pieces))
        return jnp.repeat(jnp.exp(steps), dims[dim] // parts).reshape((-1,) + (1,) * (len(dims) - dim - 1))

    factor_of = one(*pieces[0])
    for cut in pieces[1:]:
        factor_of = factor_of * one(*cut)
    return factor_of


def gaussian(own_key, extent, spread, reach, shards=(), kind=jnp.bfloat16):
    result = jax.random.normal(own_key, extent, jnp.float32) * spread
    if len(shards) > 0:
        result = block_levels(own_key, extent, shards, -0.22, 0.18) * result
    return jnp.clip(result, min=-reach, max=reach).astype(kind)


def setup_inputs(seed: int = 0) -> dict:
    splits = jax.random.split(jax.random.key(seed), 14)
    latents = gaussian(splits[0], (FRAMES, C, TOKENS), 1.0, 6.0, ((0, 16), (2, 16)), jnp.float32)
    step_index = draw_step_index(jax.random.fold_in(splits[13], 71), 0)
    levels = draw_levels(jax.random.fold_in(splits[13], 71), 0)
    modulation = gaussian(splits[3], (STEPS, 5, D), 0.5, 4.0, (), jnp.float32)
    embed_weight = gaussian(splits[4], (C, D), C ** -0.5, 1.5)
    position = gaussian(splits[5], (TOKENS, D), 0.5, 3.0, ((0, 16),))
    qkv_weight = gaussian(splits[6], (D, 3 * D), D ** -0.5, 0.1875)
    q_gain = jnp.clip(jnp.exp(jax.random.uniform(splits[7], (HD,), jnp.float32, math.log(1.0), math.log(2.5))), 1.0, 2.5)
    k_gain = jnp.clip(jnp.exp(jax.random.uniform(splits[8], (HD,), jnp.float32, math.log(1.0), math.log(2.5))), 1.0, 2.5)
    text_kv = gaussian(splits[9], (2, TXT, D), 1.0, 6.0, ((2, 16),))
    out_weight = gaussian(splits[10], (D, D), D ** -0.5, 0.1875)
    final_weight = gaussian(splits[11], (D, C), D ** -0.5, 0.1875)
    new_noise = gaussian(splits[12], (C, TOKENS), 1.0, 6.0, ((1, 16),), jnp.float32)
    return {"latents": latents, "step_index": step_index, "levels": levels, "modulation": modulation, "embed_weight": embed_weight, "position": position, "qkv_weight": qkv_weight, "q_gain": q_gain, "k_gain": k_gain, "text_kv": text_kv, "out_weight": out_weight, "final_weight": final_weight, "new_noise": new_noise}


EPSILON = 1e-06

def layer_norm(values):
    center = values - lax.optimization_barrier(jnp.mean(values, axis=-1, keepdims=True))
    return center * lax.rsqrt(lax.optimization_barrier(jnp.mean(center * center, axis=-1, keepdims=True)) + EPSILON)

def head_norm(values, gain_vector):
    widened = values.astype(jnp.float32)
    scaled = widened * lax.rsqrt(lax.optimization_barrier(jnp.mean(widened * widened, axis=-1, keepdims=True)) + EPSILON) * gain_vector
    return scaled.astype(jnp.bfloat16)

def attend_one(head_args):
    queries, keys_all, values_all, text_keys, text_values = head_args
    factor = 1.0 / math.sqrt(queries.shape[-1])
    scores = jnp.dot(queries, keys_all.T, preferred_element_type=jnp.float32) * factor
    weights = jnp.exp(scores)
    numerator = jnp.dot(weights.astype(jnp.bfloat16), values_all, preferred_element_type=jnp.float32)
    own_part = numerator / lax.optimization_barrier(jnp.sum(weights, axis=-1, keepdims=True))
    text_scores = jnp.dot(queries, text_keys.T, preferred_element_type=jnp.float32) * factor
    text_weights = jnp.exp(text_scores)
    text_numerator = jnp.dot(text_weights.astype(jnp.bfloat16), text_values, preferred_element_type=jnp.float32)
    return own_part + text_numerator / lax.optimization_barrier(jnp.sum(text_weights, axis=-1, keepdims=True))

def reference(latents, step_index, levels, modulation, embed_weight, position, qkv_weight, q_gain, k_gain, text_kv, out_weight, final_weight, new_noise):
    highest = lax.Precision.HIGHEST
    select = (step_index[:, None] == jnp.arange(STEPS, dtype=jnp.int32)[None, :]).astype(jnp.float32)
    frame_mods = jnp.dot(select, modulation.reshape(STEPS, 5 * D), precision=highest).reshape(FRAMES, 5, 1, D)
    level_low = jnp.dot(select, levels[:STEPS], precision=highest)
    level_high = jnp.dot(select, levels[1:], precision=highest)
    hidden = jnp.einsum('fcn,cd->fnd', latents, embed_weight.astype(jnp.float32), precision=highest)
    hidden = hidden + position.astype(jnp.float32)[None]
    normed = (layer_norm(hidden) * (1.0 + frame_mods[:, 1]) + frame_mods[:, 0]).astype(jnp.bfloat16)
    projected = jnp.dot(normed.reshape(FRAMES * TOKENS, D), qkv_weight, preferred_element_type=jnp.float32)
    projected = projected.astype(jnp.bfloat16).reshape(FRAMES, TOKENS, 3, HEADS, HD)
    query_heads = jnp.moveaxis(head_norm(projected[:, :, 0], q_gain), 2, 1)
    key_heads = jnp.moveaxis(head_norm(projected[:, :, 1], k_gain), 2, 1)
    value_heads = jnp.moveaxis(projected[:, :, 2], 2, 1)
    text_keys = jnp.moveaxis(head_norm(text_kv[0].reshape(TXT, HEADS, HD), k_gain), 1, 0)
    text_values = jnp.moveaxis(text_kv[1].reshape(TXT, HEADS, HD), 1, 0)

    def per_frame(frame_args):
        frame_q, frame_k, frame_v = frame_args
        return lax.map(attend_one, (frame_q, frame_k, frame_v, text_keys, text_values))
    mixture = lax.map(per_frame, (query_heads, key_heads, value_heads))
    attention = jnp.moveaxis(mixture, 1, 2).reshape(FRAMES, TOKENS, D).astype(jnp.bfloat16)
    branch = jnp.dot(attention.reshape(FRAMES * TOKENS, D), out_weight, preferred_element_type=jnp.float32).reshape(FRAMES, TOKENS, D)
    hidden_two = hidden + frame_mods[:, 2] * branch
    normed_two = (layer_norm(hidden_two) * (1.0 + frame_mods[:, 4]) + frame_mods[:, 3]).astype(jnp.bfloat16)
    velocity = jnp.einsum('fnd,dc->fcn', normed_two.astype(jnp.float32), final_weight.astype(jnp.float32))
    updated = latents + velocity * (level_high - level_low)[:, None, None]
    advanced = jnp.concatenate([updated[1:], new_noise[None]], axis=0)
    return (advanced, velocity)
```

```python
import functools
import math

import jax
import jax.numpy as jnp
from jax import lax
from jax.experimental import pallas as pl
from jax.experimental.pallas import tpu as pltpu
from jax.sharding import PartitionSpec as P

F32, BF = jnp.float32, jnp.bfloat16
MESH = pl.DeviceIdType.MESH
EPS = 1e-6
D, H, HD, C, TXT, HP = 1152, 16, 72, 16, 128, 80
ROWS = TXT + 16
CUT = 64
PARTS = ((0, CUT), (CUT, ROWS - CUT))


def nn(a, b):
    return lax.dot_general(a, b, (((1,), (0,)), ((), ())), preferred_element_type=F32)


def nt(a, b):
    return lax.dot_general(a, b, (((1,), (1,)), ((), ())), preferred_element_type=F32)


def tn(a, b):
    return lax.dot_general(a, b, (((0,), (0,)), ((), ())), preferred_element_type=F32)


def split3(x):
    a = x.astype(BF)
    r = x - a.astype(F32)
    b = r.astype(BF)
    c = (r - b.astype(F32)).astype(BF)
    return jnp.concatenate([a, b, c], axis=0)


def head_norm(rows, gain):
    ss = jnp.sum(rows * rows, axis=0, keepdims=True) * (1.0 / HD)
    return rows * lax.rsqrt(ss + EPS) * gain


def kernel(
    latx, posx, mod, levels, gains, ew, fw, noise, wqkv_hbm, wo_hbm,
    adv, vel,
    pos, lat, wqkv, wo, wt, wot, e3, mods, modsT, x, kT, vT, q, tk, tv, att, attb, hid, ubuf, vbuf,
    w_sem, own_sem, pos_send, pos_recv, lat_send, lat_recv, kv_send, kv_recv, tx_send, tx_recv,
    out_send, out_recv,
):
    qd, sq = lax.axis_index("queue"), lax.axis_index("seq")
    c = lax.rem(qd, 2)
    y = lax.rem(qd // 2, 4)
    z = (qd // 8) * 4 + sq // 4
    zl, xx = sq // 4, lax.rem(sq, 4)
    h = zl // 2
    rz = lax.rem(zl, 2)
    partner = (qd + 1 - 2 * c, sq)
    frame = sq // 2
    part = lax.rem(sq, 2)
    base = qd - c

    def at_z(step):
        zz = lax.rem(z + step + 8, 8)
        return ((zz // 4) * 8 + y * 2 + c, lax.rem(zz, 4) * 4 + xx)

    def at_x(step):
        return (qd, zl * 4 + lax.rem(xx + step, 4))

    def weights(k):
        if k < 3:
            cols = pl.ds(k * D, D)
            return pltpu.make_async_copy(wqkv_hbm.at[:, cols], wqkv.at[:, cols], w_sem.at[k])
        return pltpu.make_async_copy(wo_hbm, wo, w_sem.at[3])

    for k in range(4):
        weights(k).start()

    def rows_of(ref, color):
        low, size = PARTS[color]
        return ref.at[pl.ds(low, size), :]

    def send_block(src, slot, color, target, number):
        return pltpu.make_async_remote_copy(
            src_ref=rows_of(src, color),
            dst_ref=rows_of(pos.at[slot], color),
            send_sem=pos_send.at[number],
            recv_sem=pos_recv.at[slot, color],
            device_id=target,
            device_id_type=MESH,
        )

    def block_wait(slot, color):
        dst = rows_of(pos.at[slot], color)
        pltpu.make_async_copy(dst, dst, pos_recv.at[slot, color]).wait()

    own_slot = rz * 4 + xx
    mine = c == h
    far = 2 - 4 * lax.rem(xx, 2)

    def own_copy():
        return pltpu.make_async_copy(posx, pos.at[own_slot], own_sem.at[0])

    def first_sends():
        made = []
        for k in range(1, 4):
            made.append(send_block(posx, own_slot, 0, at_x(k), k - 1))
        for k, step in enumerate((1, -1, far)):
            made.append(send_block(posx, own_slot, 1, at_z(step), 3 + k))
        for k, step in enumerate((1, -1, far)):
            made.append(send_block(posx, own_slot, 0, at_z(step), 6 + k))
        for k in range(1, 4):
            made.append(send_block(posx, own_slot, 1, at_x(k), 9 + k - 1))
        return made

    @pl.when(mine)
    def _():
        for copy in first_sends():
            copy.start()
        own_copy().start()

    lat_slot = lax.rem(sq, 8)

    def lat_target(n):
        return base + sq // 8, 8 * c + n

    def lat_copy(n):
        return pltpu.make_async_remote_copy(
            src_ref=latx.at[n // 2], dst_ref=lat.at[lat_slot], send_sem=lat_send.at[n],
            recv_sem=lat_recv.at[lat_slot], device_id=lat_target(n), device_id_type=MESH)

    def lat_local(n):
        return pltpu.make_async_copy(latx.at[n // 2], lat.at[lat_slot], lat_recv.at[lat_slot])

    for n in range(8):
        to_q, to_s = lat_target(n)
        away = jnp.logical_or(to_q != qd, to_s != sq)

        @pl.when(away)
        def _(n=n):
            lat_copy(n).start()

        @pl.when(jnp.logical_not(away))
        def _(n=n):
            lat_local(n).start()

    for j in range(3):
        e3[C * j : C * j + C, :] = ew[...]

    def turn(src, dst, first, count):
        def one(i, carry):
            o = pl.multiple_of(i * 128, 128)
            dst[pl.ds(o, 128), :] = src[:, pl.ds(o, 128)].T
            return carry

        lax.fori_loop(first, first + count, one, 0)

    weights(1).wait()
    turn(wqkv, wt, 9, 9)
    weights(2).wait()
    turn(wqkv, wt, 18, 9)

    def row_relays(k):
        src = lax.rem(xx + k, 4)
        slot = rz * 4 + src
        step = 2 - 4 * lax.rem(src, 2)
        return [
            send_block(pos.at[slot], slot, 0, at_z(s), 12 + 3 * (k - 1) + n)
            for n, s in enumerate((1, -1, step))
        ]

    def column_relays(r):
        slot = r * 4 + xx
        return [send_block(pos.at[slot], slot, 1, at_x(k), 21 + 3 * r + k - 1) for k in range(1, 4)]

    @pl.when(mine)
    def _():
        for k in range(1, 4):
            block_wait(rz * 4 + lax.rem(xx + k, 4), 0)
            for copy in row_relays(k):
                copy.start()

    for r in range(2):

        @pl.when(jnp.logical_not(jnp.logical_and(mine, rz == r)))
        def _(r=r):
            block_wait(r * 4 + xx, 1)
            for copy in column_relays(r):
                copy.start()

    weights(0).wait()
    turn(wqkv, wt, 0, 9)
    weights(3).wait()
    turn(wo, wot, 0, 9)

    for n in range(8):
        pltpu.make_async_copy(lat.at[n], lat.at[n], lat_recv.at[n]).wait()

    stepf = lat[0, 16:17, 0:1]
    acc = jnp.zeros((5, D), F32)
    for i in range(mod.shape[0]):
        acc = acc + jnp.where(stepf == float(i), mod[i], 0.0)
    mods[0:5, :] = acc
    mods[5:8, :] = jnp.zeros((3, D), F32)
    modsT[...] = mods[...].T
    lane = lax.broadcasted_iota(jnp.int32, levels.shape, 1).astype(F32)
    low = jnp.sum(jnp.where(lane == stepf, levels[...], 0.0), axis=1, keepdims=True)
    high = jnp.sum(jnp.where(lane == stepf + 1.0, levels[...], 0.0), axis=1, keepdims=True)
    step_size = high - low

    @pl.when(mine)
    def _():
        own_copy().wait()

    ones = (lax.broadcasted_iota(jnp.int32, (HP - HD, 256), 0) == 0).astype(F32)
    nothing = jnp.zeros((HP - HD, 256), F32)
    heads_at_once = 4
    rows_at_once = heads_at_once * HD

    def kv_copy(pair, which):
        ref = (kT, vT)[which]
        cols = pl.ds(pl.multiple_of(c * 1024 + pair * 256, 256), 256)
        return pltpu.make_async_remote_copy(
            src_ref=ref.at[:, :, cols], dst_ref=ref.at[:, :, cols], send_sem=kv_send.at[pair, which],
            recv_sem=kv_recv.at[pair, which], device_id=partner, device_id_type=MESH)

    def kv_wait(pair, which):
        ref = (kT, vT)[which]
        cols = pl.ds(pl.multiple_of((1 - c) * 1024 + pair * 256, 256), 256)
        dst = ref.at[:, :, cols]
        pltpu.make_async_copy(dst, dst, kv_recv.at[pair, which]).wait()

    def one_pair(n, carry):
        row = lax.rem(rz + n // 2, 2)
        pair = row * 2 + lax.rem(n, 2)
        for k in range(2):
            slot = pair * 2 + k
            column = lax.rem(slot, 4)

            @pl.when(jnp.logical_not(jnp.logical_and(mine, row == rz)))
            def _(slot=slot):
                block_wait(slot, 0)

            @pl.when(column != xx)
            def _(slot=slot):
                block_wait(slot, 1)

        a, b = pair * 2, pair * 2 + 1
        l3 = jnp.concatenate([split3(lat[a, 0:C]), split3(lat[b, 0:C])], axis=1)
        places = jnp.concatenate([pos[a, 0:TXT], pos[b, 0:TXT]], axis=0)
        hidden = tn(l3, e3[...]) + places.astype(F32)
        center = hidden - jnp.mean(hidden, axis=-1, keepdims=True)
        unit = center * lax.rsqrt(jnp.mean(center * center, axis=-1, keepdims=True) + EPS)
        xb = (unit * (1.0 + mods[1:2]) + mods[0:1]).astype(BF)
        x[pair] = xb
        cols = pl.ds(pl.multiple_of(c * 1024 + pair * 256, 256), 256)
        for g in range(H // heads_at_once):
            o = D + g * rows_at_once
            r = nt(wt[o : o + rows_at_once, :], xb)
            for j in range(heads_at_once):
                rows = r[j * HD : (j + 1) * HD].astype(BF).astype(F32)
                padded = jnp.concatenate([head_norm(rows, gains[1]), nothing], axis=0)
                kT[g * heads_at_once + j, :, cols] = padded.astype(BF)
        for g in range(H // heads_at_once):
            o = 2 * D + g * rows_at_once
            r = nt(wt[o : o + rows_at_once, :], xb)
            for j in range(heads_at_once):
                padded = jnp.concatenate([r[j * HD : (j + 1) * HD], ones], axis=0)
                vT[g * heads_at_once + j, :, cols] = padded.astype(BF)
        for k in range(2):
            slot = pair * 2 + k
            t = jnp.concatenate([pos[slot, TXT:ROWS, 128 * j : 128 * j + 128] for j in range(9)], axis=0)
            t = t.astype(F32)
            keys = jnp.concatenate([head_norm(t[0:HD], gains[1, :, 0:128]), nothing[:, 0:128]], axis=0)
            tk[8 * c + slot] = keys.astype(BF)
            tv[8 * c + slot] = jnp.concatenate([t[HD : 2 * HD], ones[:, 0:128]], axis=0).astype(BF)

        @pl.when(n > 0)
        def _():
            before = lax.rem(rz + (n - 1) // 2, 2) * 2 + lax.rem(n - 1, 2)
            kv_copy(before, 0).start()
            kv_copy(before, 1).start()

        return carry

    lax.fori_loop(0, 4, one_pair, 0)

    def one_query_block(n, carry):
        xb = x[part * 2 + n]
        cols = pl.ds(pl.multiple_of(n * 256, 256), 256)
        for g in range(H // heads_at_once):
            o = g * rows_at_once
            r = nt(wt[o : o + rows_at_once, :], xb)
            for j in range(heads_at_once):
                rows = r[j * HD : (j + 1) * HD].astype(BF).astype(F32)
                padded = jnp.concatenate([head_norm(rows, gains[0]), jnp.zeros((128 - HD, 256), F32)], axis=0)
                q[g * heads_at_once + j, cols, :] = padded.T.astype(BF)

        @pl.when(n == 0)
        def _():
            last = lax.rem(rz + 1, 2) * 2 + 1
            kv_copy(last, 0).start()
            kv_copy(last, 1).start()
            for which in range(2):
                tx_copy(which).start()

        return carry

    def tx_copy(which):
        ref = (tk, tv)[which]
        rows = pl.ds(8 * c, 8)
        return pltpu.make_async_remote_copy(
            src_ref=ref.at[rows], dst_ref=ref.at[rows], send_sem=tx_send.at[which],
            recv_sem=tx_recv.at[which], device_id=partner, device_id_type=MESH)

    def tx_wait(which):
        dst = (tk, tv)[which].at[pl.ds(8 * (1 - c), 8)]
        pltpu.make_async_copy(dst, dst, tx_recv.at[which]).wait()

    lax.fori_loop(0, 2, one_query_block, 0)
    for which in range(2):
        tx_wait(which)
        for pair in range(4):
            kv_wait(pair, which)

    def one_head(n, carry):
        made = []
        for half in range(2):
            qh = q[n, half * 256 : half * 256 + 256, 0:HP]
            p = jnp.exp2(nn(qh, kT[n])).astype(BF)
            own = nt(vT[n], p)
            pt = jnp.exp2(nn(qh, tk[n])).astype(BF)
            text = nt(tv[n], pt)
            made.append(own[0:HD] / own[HD : HD + 1] + text[0:HD] / text[HD : HD + 1])
        att[pl.ds(pl.multiple_of(n * HD, 8), HD), :] = jnp.concatenate(made, axis=1)
        return carry

    lax.fori_loop(0, H, one_head, 0)

    attb[...] = att[...].astype(BF)
    for t in range(4):
        slot = part * 4 + t
        hid[:, t * 128 : t * 128 + 128] = tn(e3[...], split3(lat[slot, 0:C])) + pos[slot, 0:TXT].T.astype(F32)
    for g in range(2):
        r = slice(g * 576, g * 576 + 576)
        hid[r, :] = hid[r, :] + modsT[r, 2:3] * nn(wot[r, :], attb[...])
    hidden = hid[...]
    center = hidden - jnp.sum(hidden, axis=0, keepdims=True) * (1.0 / D)
    scale = lax.rsqrt(jnp.sum(center * center, axis=0, keepdims=True) * (1.0 / D) + EPS)
    xb = (center * scale * (1.0 + modsT[:, 4:5]) + modsT[:, 3:4]).astype(BF)
    speed = tn(fw[...], xb)
    for t in range(4):
        piece = speed[:, t * 128 : t * 128 + 128]
        vbuf[t] = piece
        ubuf[t] = lat[part * 4 + t, 0:C] + step_size * piece

    whole = (qd // 2) * 8 + frame
    before = jnp.maximum(whole - 1, 0)

    def out_copy(which, t):
        src, dst, place = ((vbuf, vel, whole), (ubuf, adv, before))[which]
        there = lax.rem(place, 4)
        return pltpu.make_async_remote_copy(
            src_ref=src.at[t], dst_ref=dst.at[there], send_sem=out_send.at[which, t],
            recv_sem=out_recv.at[which, there],
            device_id=(place // 4, 8 * c + 4 * part + t), device_id_type=MESH)

    def out_local(which, t):
        src, dst, place = ((vbuf, vel, whole), (ubuf, adv, before))[which]
        there = lax.rem(place, 4)
        return pltpu.make_async_copy(src.at[t], dst.at[there], out_recv.at[which, there])

    def out_cases(which, t):
        place = (whole, before)[which]
        here = jnp.logical_and(place // 4 == qd, 8 * c + 4 * part + t == sq)
        away = jnp.logical_not(here)
        if which == 1:
            here = jnp.logical_and(here, whole > 0)
            away = jnp.logical_and(away, whole > 0)
        return here, away

    for which in range(2):
        for t in range(4):
            here, away = out_cases(which, t)

            @pl.when(away)
            def _(which=which, t=t):
                out_copy(which, t).start()

            @pl.when(here)
            def _(which=which, t=t):
                out_local(which, t).start()

    @pl.when(mine)
    def _():
        for copy in first_sends():
            copy.wait_send()
        for k in range(1, 4):
            for copy in row_relays(k):
                copy.wait_send()

    for r in range(2):

        @pl.when(jnp.logical_not(jnp.logical_and(mine, rz == r)))
        def _(r=r):
            for copy in column_relays(r):
                copy.wait_send()

    for n in range(8):
        to_q, to_s = lat_target(n)

        @pl.when(jnp.logical_or(to_q != qd, to_s != sq))
        def _(n=n):
            lat_copy(n).wait_send()

    for which in range(2):
        tx_copy(which).wait_send()
        for pair in range(4):
            kv_copy(pair, which).wait_send()
        for t in range(4):

            @pl.when(out_cases(which, t)[1])
            def _(which=which, t=t):
                out_copy(which, t).wait_send()

    for n in range(4):
        pltpu.make_async_copy(vel.at[n], vel.at[n], out_recv.at[0, n]).wait()
    for n in range(3):
        pltpu.make_async_copy(adv.at[n], adv.at[n], out_recv.at[1, n]).wait()

    @pl.when(qd < 15)
    def _():
        pltpu.make_async_copy(adv.at[3], adv.at[3], out_recv.at[1, 3]).wait()

    @pl.when(qd == 15)
    def _():
        adv[3] = noise[...]


def body(
    latents, step_index, levels, modulation, embed_weight, position, qkv_weight, q_gain, k_gain,
    text_kv, out_weight, final_weight, new_noise,
):
    frames = latents.shape[0]
    steps = jnp.broadcast_to(step_index.astype(F32)[:, None, None], (frames, 8, 128))
    latx = jnp.concatenate([latents, steps], axis=1)
    text = jnp.swapaxes(text_kv, 1, 2).reshape(9, 16, TXT)
    posx = jnp.concatenate([position, jnp.swapaxes(text, 0, 1).reshape(16, D)], axis=0)
    fold = math.log2(math.e) / math.sqrt(HD)
    gains = jnp.broadcast_to(jnp.stack([q_gain * fold, k_gain])[:, :, None], (2, HD, 256))
    inner = pl.BlockSpec(memory_space=pltpu.VMEM)
    outer = pl.BlockSpec(memory_space=pl.ANY)
    dma = pltpu.SemaphoreType.DMA
    return pl.pallas_call(
        kernel,
        out_shape=(jax.ShapeDtypeStruct(latents.shape, F32),) * 2,
        in_specs=[inner] * 8 + [outer] * 2,
        out_specs=(inner, inner),
        scratch_shapes=[
            pltpu.VMEM((8, ROWS, D), BF),
            pltpu.VMEM((8, 24, 128), F32),
            pltpu.VMEM((D, 3 * D), BF),
            pltpu.VMEM((D, D), BF),
            pltpu.VMEM((3 * D, D), BF),
            pltpu.VMEM((D, D), BF),
            pltpu.VMEM((3 * C, D), BF),
            pltpu.VMEM((8, D), F32),
            pltpu.VMEM((D, 8), F32),
            pltpu.VMEM((4, 256, D), BF),
            pltpu.VMEM((H, HP, 2048), BF),
            pltpu.VMEM((H, HP, 2048), BF),
            pltpu.VMEM((H, 512, 128), BF),
            pltpu.VMEM((H, HP, TXT), BF),
            pltpu.VMEM((H, HP, TXT), BF),
            pltpu.VMEM((D, 512), F32),
            pltpu.VMEM((D, 512), BF),
            pltpu.VMEM((D, 512), F32),
            pltpu.VMEM((4, C, 128), F32),
            pltpu.VMEM((4, C, 128), F32),
            dma((4,)),
            dma((1,)),
            dma((27,)),
            dma((8, 2)),
            dma((8,)),
            dma((8,)),
            dma((4, 2)),
            dma((4, 2)),
            dma((2,)),
            dma((2,)),
            dma((2, 4)),
            dma((2, 4)),
        ],
        compiler_params=pltpu.CompilerParams(
            vmem_limit_bytes=62 * 1024 * 1024, has_side_effects=True
        ),
        name="denoise",
    )(
        latx, posx, modulation, levels[None, :], gains, embed_weight, final_weight, new_noise,
        qkv_weight, out_weight,
    )


def solution(mesh):
    in_specs = (
        P("queue", None, "seq"), P("queue"), P(), P(), P(), P("seq", None), P(), P(), P(),
        P(None, None, "seq"), P(), P(), P(None, "seq"),
    )
    out_specs = (P("queue", None, "seq"), P("queue", None, "seq"))
    return jax.shard_map(body, mesh=mesh, in_specs=in_specs, out_specs=out_specs, check_vma=False)
```

```python
import functools
import math

import jax
import jax.numpy as jnp
from jax import lax
from jax.experimental import pallas as pl
from jax.experimental.pallas import tpu as pltpu
from jax.sharding import PartitionSpec as P

F32, BF = jnp.float32, jnp.bfloat16
MESH = pl.DeviceIdType.MESH
EPS = 1e-6
D, H, HD, C, TXT, HP = 1152, 16, 72, 16, 128, 80
ROWS = TXT + 16
CUT = 64
PARTS = ((0, CUT), (CUT, ROWS - CUT))


def nn(a, b):
    return lax.dot_general(a, b, (((1,), (0,)), ((), ())), preferred_element_type=F32)


def nt(a, b):
    return lax.dot_general(a, b, (((1,), (1,)), ((), ())), preferred_element_type=F32)


def tn(a, b):
    return lax.dot_general(a, b, (((0,), (0,)), ((), ())), preferred_element_type=F32)


def split3(x):
    a = x.astype(BF)
    r = x - a.astype(F32)
    b = r.astype(BF)
    c = (r - b.astype(F32)).astype(BF)
    return jnp.concatenate([a, b, c], axis=0)


def head_norm(rows, gain):
    ss = jnp.sum(rows * rows, axis=0, keepdims=True) * (1.0 / HD)
    return rows * lax.rsqrt(ss + EPS) * gain


def kernel(
    latents, steps, posin, text, mod, levels, qg, kg, ew, fw, noise, wqkv_hbm, wo_hbm,
    out,
    pos, lat, latx, gains8, gains, wqkv, wo, wt, wot, e3, mods, modsT, x, kT, vT, q, tk, tv, att, attb, hid, ubuf, vbuf,
    w_sem, own_sem, pos_send, pos_recv, lat_send, lat_recv, kv_send, kv_recv, tx_send, tx_recv,
    out_send, out_recv,
):
    qd, sq = lax.axis_index("queue"), lax.axis_index("seq")
    c = lax.rem(qd, 2)
    y = lax.rem(qd // 2, 4)
    z = (qd // 8) * 4 + sq // 4
    zl, xx = sq // 4, lax.rem(sq, 4)
    h = zl // 2
    rz = lax.rem(zl, 2)
    partner = (qd + 1 - 2 * c, sq)
    frame = sq // 2
    part = lax.rem(sq, 2)
    base = qd - c

    def at_z(step):
        zz = lax.rem(z + step + 8, 8)
        return ((zz // 4) * 8 + y * 2 + c, lax.rem(zz, 4) * 4 + xx)

    def at_x(step):
        return (qd, zl * 4 + lax.rem(xx + step + 4, 4))

    def weights(k):
        if k < 3:
            cols = pl.ds(k * D, D)
            return pltpu.make_async_copy(wqkv_hbm.at[:, cols], wqkv.at[:, cols], w_sem.at[k])
        return pltpu.make_async_copy(wo_hbm, wo, w_sem.at[3])

    for k in range(4):
        weights(k).start()

    barrier = pltpu.get_barrier_semaphore()

    def greet(target):
        pl.semaphore_signal(barrier, inc=1, device_id=target, device_id_type=MESH)

    for target in (at_x(1), at_x(-1), at_z(1), at_z(-1), partner):
        greet(target)
    for n in range(8):

        @pl.when(jnp.logical_or(base + h != qd, 8 * c + n != sq))
        def _(n=n):
            greet((base + h, 8 * c + n))

    after = (qd + 1) // 2 * 2

    @pl.when(qd < 15)
    def _():
        greet((after + h, 8 * lax.rem(qd + 1, 2) + lax.rem(sq, 8) // 4))

    starts = jnp.logical_or(sq // 2 == 4, jnp.logical_and(sq // 2 == 0, base > 0))
    pl.semaphore_wait(barrier, 13 - jnp.where(c == h, 1, 0) + jnp.where(starts, 4, 0))

    def rows_of(ref, color):
        low, size = PARTS[color]
        return ref.at[pl.ds(low, size), :]

    def send_block(src, slot, color, target, number):
        return pltpu.make_async_remote_copy(
            src_ref=rows_of(src, color),
            dst_ref=rows_of(pos.at[slot], color),
            send_sem=pos_send.at[number],
            recv_sem=pos_recv.at[slot, color],
            device_id=target,
            device_id_type=MESH,
        )

    def block_wait(slot, color):
        dst = rows_of(pos.at[slot], color)
        pltpu.make_async_copy(dst, dst, pos_recv.at[slot, color]).wait()

    own_slot = rz * 4 + xx
    mine = c == h
    odd = lax.rem(xx, 2)

    def own_copies():
        made = [pltpu.make_async_copy(posin, pos.at[own_slot, pl.ds(0, TXT), :], own_sem.at[9])]
        for j in range(9):
            dst = pos.at[own_slot, pl.ds(TXT, 16), pl.ds(128 * j, 128)]
            made.append(pltpu.make_async_copy(text.at[j], dst, own_sem.at[j]))
        return made

    def first_sends(color):
        src = posin if color == 0 else pos.at[own_slot]
        targets = (at_x(1), at_x(-1), at_z(1), at_z(-1))
        return [send_block(src, own_slot, color, t, 4 * color + k) for k, t in enumerate(targets)]

    def row_relays(k):
        slot = rz * 4 + lax.rem(xx + k, 4)
        return [send_block(pos.at[slot], slot, 0, at_z(s), 8 + 2 * (k - 1) + n) for n, s in enumerate((1, -1))]

    def row_hop():
        step = 2 * odd - 1
        slot = rz * 4 + lax.rem(xx - step + 4, 4)
        return send_block(pos.at[slot], slot, 0, at_x(step), 14)

    def column_relays(r):
        slot = r * 4 + xx
        return [send_block(pos.at[slot], slot, 1, at_x(s), 15 + 2 * r + n) for n, s in enumerate((1, -1))]

    def delta(row):
        return lax.rem(2 * c + row - zl + 4, 4)

    def near(row):
        return lax.rem(delta(row), 2) == 1

    def z_hop(slot, color, row, number):
        return send_block(pos.at[slot], slot, color, at_z(delta(row) - 2), number)

    def column_hop_due(r):
        return jnp.logical_and(near(r), odd == jnp.where(delta(r) == 3, 0, 1))

    def row_hop_slot(r, k):
        return r * 4 + 2 * k + jnp.where(delta(r) == 3, 0, 1)

    def across_slot(r):
        return r * 4 + lax.rem(xx + (3, 1)[r], 4)

    def across_slot_of(row):
        return row * 4 + lax.rem(xx + 3 - 2 * row, 4)

    def across_hop(r):
        slot = across_slot(r)
        return send_block(pos.at[slot], slot, 1, at_x((1, -1)[r]), 25 + r)

    @pl.when(mine)
    def _():
        for copy in first_sends(0):
            copy.start()
        for copy in own_copies():
            copy.start()

    for n in range(4):
        latx[n, 0:C] = latents[n]
        latx[n, C:24] = jnp.full((8, 128), steps[n].astype(F32))
    fold = math.log2(math.e) / math.sqrt(HD)
    gains8[...] = jnp.zeros((8, 128), F32)
    gains8[0:1, 0:HD] = qg[...] * fold
    gains8[1:2, 0:HD] = kg[...]
    columns = gains8[...].T
    for k in range(2):
        gains[k] = jnp.broadcast_to(columns[0:HD, k : k + 1], (HD, 256))

    @pl.when(mine)
    def _():
        for copy in own_copies():
            copy.wait()
        for copy in first_sends(1):
            copy.start()

    lat_slot = lax.rem(sq, 8)

    def lat_target(n):
        return base + sq // 8, 8 * c + n

    def lat_copy(n):
        return pltpu.make_async_remote_copy(
            src_ref=latx.at[n // 2], dst_ref=lat.at[lat_slot], send_sem=lat_send.at[n],
            recv_sem=lat_recv.at[lat_slot], device_id=lat_target(n), device_id_type=MESH)

    def lat_local(n):
        return pltpu.make_async_copy(latx.at[n // 2], lat.at[lat_slot], lat_recv.at[lat_slot])

    for n in range(8):
        to_q, to_s = lat_target(n)
        away = jnp.logical_or(to_q != qd, to_s != sq)

        @pl.when(away)
        def _(n=n):
            lat_copy(n).start()

        @pl.when(jnp.logical_not(away))
        def _(n=n):
            lat_local(n).start()

    for j in range(3):
        e3[C * j : C * j + C, :] = ew[...]

    def turn(src, dst, first, count):
        def one(i, carry):
            o = pl.multiple_of(i * 128, 128)
            dst[pl.ds(o, 128), :] = src[:, pl.ds(o, 128)].T
            return carry

        lax.fori_loop(first, first + count, one, 0)

    weights(1).wait()
    turn(wqkv, wt, 9, 9)

    @pl.when(mine)
    def _():
        for k in (1, 3):
            block_wait(rz * 4 + lax.rem(xx + k, 4), 0)
        row_hop().start()
        for k in (1, 3):
            for copy in row_relays(k):
                copy.start()

    for r in range(2):

        @pl.when(near(r))
        def _(r=r):
            block_wait(r * 4 + xx, 1)

        @pl.when(column_hop_due(r))
        def _(r=r):
            z_hop(r * 4 + xx, 1, r, 19 + r).start()

        @pl.when(near(r))
        def _(r=r):
            for copy in column_relays(r):
                copy.start()

    weights(2).wait()
    turn(wqkv, wt, 18, 9)

    @pl.when(mine)
    def _():
        block_wait(rz * 4 + lax.rem(xx + 2, 4), 0)
        for copy in row_relays(2):
            copy.start()

    for r in range(2):

        @pl.when(delta(r) == 2)
        def _(r=r):
            block_wait(r * 4 + xx, 1)
            for copy in column_relays(r):
                copy.start()

    weights(0).wait()
    turn(wqkv, wt, 0, 9)

    for r in range(2):

        @pl.when(near(r))
        def _(r=r):
            for k in range(2):
                block_wait(row_hop_slot(r, k), 0)
                z_hop(row_hop_slot(r, k), 0, r, 21 + 2 * r + k).start()

    for r in range(2):
        block_wait(across_slot(r), 1)
        across_hop(r).start()

    weights(3).wait()
    turn(wo, wot, 0, 9)

    for n in range(8):
        pltpu.make_async_copy(lat.at[n], lat.at[n], lat_recv.at[n]).wait()

    stepf = lat[0, 16:17, 0:1]
    plan = lax.broadcasted_iota(jnp.int32, mod.shape[1:], 0).astype(F32)
    for i in range(5):
        mods[i : i + 1, :] = jnp.sum(jnp.where(plan == stepf, mod[i], 0.0), axis=0, keepdims=True)
    mods[5:8, :] = jnp.zeros((3, D), F32)
    modsT[...] = mods[...].T
    lane = lax.broadcasted_iota(jnp.int32, levels.shape, 1).astype(F32)
    low = jnp.sum(jnp.where(lane == stepf, levels[...], 0.0), axis=1, keepdims=True)
    high = jnp.sum(jnp.where(lane == stepf + 1.0, levels[...], 0.0), axis=1, keepdims=True)
    step_size = high - low

    ones = (lax.broadcasted_iota(jnp.int32, (HP - HD, 256), 0) == 0).astype(F32)
    nothing = jnp.zeros((HP - HD, 256), F32)
    heads_at_once = 4
    rows_at_once = heads_at_once * HD

    def kv_copy(pair, which):
        ref = (kT, vT)[which]
        cols = pl.ds(pl.multiple_of(c * 1024 + pair * 256, 256), 256)
        return pltpu.make_async_remote_copy(
            src_ref=ref.at[:, :, cols], dst_ref=ref.at[:, :, cols], send_sem=kv_send.at[pair, which],
            recv_sem=kv_recv.at[pair, which], device_id=partner, device_id_type=MESH)

    def kv_wait(pair, which):
        ref = (kT, vT)[which]
        cols = pl.ds(pl.multiple_of((1 - c) * 1024 + pair * 256, 256), 256)
        dst = ref.at[:, :, cols]
        pltpu.make_async_copy(dst, dst, kv_recv.at[pair, which]).wait()

    def nth_row(n):
        return lax.rem(jnp.where(mine, rz, 1 - rz) + n // 2, 2)

    def one_pair(n, carry):
        row = nth_row(n)
        pair = row * 2 + lax.rem(n, 2)
        for k in range(2):
            slot = pair * 2 + k
            column = lax.rem(slot, 4)

            passed = jnp.where(delta(row) == 3, 0, jnp.where(delta(row) == 1, 1, 2))

            @pl.when(jnp.logical_and(delta(row) > 0, lax.rem(slot, 2) != passed))
            def _(slot=slot):
                block_wait(slot, 0)

            @pl.when(jnp.logical_and(column != xx, slot != across_slot_of(row)))
            def _(slot=slot):
                block_wait(slot, 1)

        a, b = pair * 2, pair * 2 + 1
        l3 = jnp.concatenate([split3(lat[a, 0:C]), split3(lat[b, 0:C])], axis=1)
        places = jnp.concatenate([pos[a, 0:TXT], pos[b, 0:TXT]], axis=0)
        hidden = tn(l3, e3[...]) + places.astype(F32)
        center = hidden - jnp.mean(hidden, axis=-1, keepdims=True)
        unit = center * lax.rsqrt(jnp.mean(center * center, axis=-1, keepdims=True) + EPS)
        xb = (unit * (1.0 + mods[1:2]) + mods[0:1]).astype(BF)
        x[pair] = xb
        cols = pl.ds(pl.multiple_of(c * 1024 + pair * 256, 256), 256)
        for g in range(H // heads_at_once):
            o = D + g * rows_at_once
            r = nt(wt[o : o + rows_at_once, :], xb)
            for j in range(heads_at_once):
                rows = r[j * HD : (j + 1) * HD].astype(BF).astype(F32)
                padded = jnp.concatenate([head_norm(rows, gains[1]), nothing], axis=0)
                kT[g * heads_at_once + j, :, cols] = padded.astype(BF)
        for g in range(H // heads_at_once):
            o = 2 * D + g * rows_at_once
            r = nt(wt[o : o + rows_at_once, :], xb)
            for j in range(heads_at_once):
                padded = jnp.concatenate([r[j * HD : (j + 1) * HD], ones], axis=0)
                vT[g * heads_at_once + j, :, cols] = padded.astype(BF)
        for k in range(2):
            slot = pair * 2 + k
            t = jnp.concatenate([pos[slot, TXT:ROWS, 128 * j : 128 * j + 128] for j in range(9)], axis=0)
            t = t.astype(F32)
            keys = jnp.concatenate([head_norm(t[0:HD], gains[1, :, 0:128]), nothing[:, 0:128]], axis=0)
            tk[8 * c + slot] = keys.astype(BF)
            tv[8 * c + slot] = jnp.concatenate([t[HD : 2 * HD], ones[:, 0:128]], axis=0).astype(BF)

        @pl.when(n > 0)
        def _():
            before = nth_row(n - 1) * 2 + lax.rem(n - 1, 2)
            kv_copy(before, 0).start()
            kv_copy(before, 1).start()

        return carry

    lax.fori_loop(0, 4, one_pair, 0)

    def one_query_block(n, carry):
        xb = x[part * 2 + n]
        cols = pl.ds(pl.multiple_of(n * 256, 256), 256)
        for g in range(H // heads_at_once):
            o = g * rows_at_once
            r = nt(wt[o : o + rows_at_once, :], xb)
            for j in range(heads_at_once):
                rows = r[j * HD : (j + 1) * HD].astype(BF).astype(F32)
                padded = jnp.concatenate([head_norm(rows, gains[0]), jnp.zeros((128 - HD, 256), F32)], axis=0)
                q[g * heads_at_once + j, cols, :] = padded.T.astype(BF)

        @pl.when(n == 0)
        def _():
            last = nth_row(3) * 2 + 1
            kv_copy(last, 0).start()
            kv_copy(last, 1).start()
            for which in range(2):
                tx_copy(which).start()

        return carry

    def tx_copy(which):
        ref = (tk, tv)[which]
        rows = pl.ds(8 * c, 8)
        return pltpu.make_async_remote_copy(
            src_ref=ref.at[rows], dst_ref=ref.at[rows], send_sem=tx_send.at[which],
            recv_sem=tx_recv.at[which], device_id=partner, device_id_type=MESH)

    def tx_wait(which):
        dst = (tk, tv)[which].at[pl.ds(8 * (1 - c), 8)]
        pltpu.make_async_copy(dst, dst, tx_recv.at[which]).wait()

    lax.fori_loop(0, 2, one_query_block, 0)
    for which in range(2):
        tx_wait(which)
        for pair in range(4):
            kv_wait(pair, which)

    def one_head(n, carry):
        made = []
        for half in range(2):
            qh = q[n, half * 256 : half * 256 + 256, 0:HP]
            p = jnp.exp2(nn(qh, kT[n])).astype(BF)
            own = nt(vT[n], p)
            pt = jnp.exp2(nn(qh, tk[n])).astype(BF)
            text = nt(tv[n], pt)
            made.append(own[0:HD] / own[HD : HD + 1] + text[0:HD] / text[HD : HD + 1])
        att[pl.ds(pl.multiple_of(n * HD, 8), HD), :] = jnp.concatenate(made, axis=1)
        return carry

    lax.fori_loop(0, H, one_head, 0)

    attb[...] = att[...].astype(BF)
    for t in range(4):
        slot = part * 4 + t
        hid[:, t * 128 : t * 128 + 128] = tn(e3[...], split3(lat[slot, 0:C])) + pos[slot, 0:TXT].T.astype(F32)
    for g in range(2):
        r = slice(g * 576, g * 576 + 576)
        hid[r, :] = hid[r, :] + modsT[r, 2:3] * nn(wot[r, :], attb[...])
    hidden = hid[...]
    center = hidden - jnp.sum(hidden, axis=0, keepdims=True) * (1.0 / D)
    scale = lax.rsqrt(jnp.sum(center * center, axis=0, keepdims=True) * (1.0 / D) + EPS)
    xb = (center * scale * (1.0 + modsT[:, 4:5]) + modsT[:, 3:4]).astype(BF)
    speed = nn(fw[...], xb)
    for t in range(4):
        piece = speed[:, t * 128 : t * 128 + 128]
        vbuf[t] = piece
        ubuf[t] = lat[part * 4 + t, 0:C] + step_size * piece

    whole = (qd // 2) * 8 + frame
    before = jnp.maximum(whole - 1, 0)

    def out_copy(which, t):
        src, dst, place = ((vbuf, 0, whole), (ubuf, 1, before))[which]
        there = lax.rem(place, 4)
        return pltpu.make_async_remote_copy(
            src_ref=src.at[t], dst_ref=out.at[dst, there], send_sem=out_send.at[which, t],
            recv_sem=out_recv.at[which, there],
            device_id=(place // 4, 8 * c + 4 * part + t), device_id_type=MESH)

    def out_local(which, t):
        src, dst, place = ((vbuf, 0, whole), (ubuf, 1, before))[which]
        there = lax.rem(place, 4)
        return pltpu.make_async_copy(src.at[t], out.at[dst, there], out_recv.at[which, there])

    def out_cases(which, t):
        place = (whole, before)[which]
        here = jnp.logical_and(place // 4 == qd, 8 * c + 4 * part + t == sq)
        away = jnp.logical_not(here)
        if which == 1:
            here = jnp.logical_and(here, whole > 0)
            away = jnp.logical_and(away, whole > 0)
        return here, away

    for which in range(2):
        for t in range(4):
            here, away = out_cases(which, t)

            @pl.when(away)
            def _(which=which, t=t):
                out_copy(which, t).start()

            @pl.when(here)
            def _(which=which, t=t):
                out_local(which, t).start()

    @pl.when(mine)
    def _():
        for color in range(2):
            for copy in first_sends(color):
                copy.wait_send()
        row_hop().wait_send()
        for k in range(1, 4):
            for copy in row_relays(k):
                copy.wait_send()

    for r in range(2):

        @pl.when(delta(r) > 0)
        def _(r=r):
            for copy in column_relays(r):
                copy.wait_send()

        @pl.when(column_hop_due(r))
        def _(r=r):
            z_hop(r * 4 + xx, 1, r, 19 + r).wait_send()

        @pl.when(near(r))
        def _(r=r):
            for k in range(2):
                z_hop(row_hop_slot(r, k), 0, r, 21 + 2 * r + k).wait_send()

        across_hop(r).wait_send()

    for n in range(8):
        to_q, to_s = lat_target(n)

        @pl.when(jnp.logical_or(to_q != qd, to_s != sq))
        def _(n=n):
            lat_copy(n).wait_send()

    for which in range(2):
        tx_copy(which).wait_send()
        for pair in range(4):
            kv_copy(pair, which).wait_send()
        for t in range(4):

            @pl.when(out_cases(which, t)[1])
            def _(which=which, t=t):
                out_copy(which, t).wait_send()

    for which, count in ((0, 4), (1, 3)):
        for n in range(count):
            dst = out.at[which, n]
            pltpu.make_async_copy(dst, dst, out_recv.at[which, n]).wait()

    @pl.when(qd < 15)
    def _():
        dst = out.at[1, 3]
        pltpu.make_async_copy(dst, dst, out_recv.at[1, 3]).wait()

    @pl.when(qd == 15)
    def _():
        out[1, 3] = noise[...]


def body(
    latents, step_index, levels, modulation, embed_weight, position, qkv_weight, q_gain, k_gain,
    text_kv, out_weight, final_weight, new_noise,
):
    text = jnp.swapaxes(text_kv, 1, 2).reshape(9, 16, TXT)
    inner = pl.BlockSpec(memory_space=pltpu.VMEM)
    outer = pl.BlockSpec(memory_space=pl.ANY)
    dma = pltpu.SemaphoreType.DMA
    scalars = pl.BlockSpec(memory_space=pltpu.SMEM)
    both = pl.pallas_call(
        kernel,
        out_shape=jax.ShapeDtypeStruct((2,) + latents.shape, F32),
        in_specs=[inner, scalars] + [inner] * 9 + [outer] * 2,
        out_specs=inner,
        scratch_shapes=[
            pltpu.VMEM((8, ROWS, D), BF),
            pltpu.VMEM((8, 24, 128), F32),
            pltpu.VMEM((4, 24, 128), F32),
            pltpu.VMEM((8, 128), F32),
            pltpu.VMEM((2, HD, 256), F32),
            pltpu.VMEM((D, 3 * D), BF),
            pltpu.VMEM((D, D), BF),
            pltpu.VMEM((3 * D, D), BF),
            pltpu.VMEM((D, D), BF),
            pltpu.VMEM((3 * C, D), BF),
            pltpu.VMEM((8, D), F32),
            pltpu.VMEM((D, 8), F32),
            pltpu.VMEM((4, 256, D), BF),
            pltpu.VMEM((H, HP, 2048), BF),
            pltpu.VMEM((H, HP, 2048), BF),
            pltpu.VMEM((H, 512, 128), BF),
            pltpu.VMEM((H, HP, TXT), BF),
            pltpu.VMEM((H, HP, TXT), BF),
            pltpu.VMEM((D, 512), F32),
            pltpu.VMEM((D, 512), BF),
            pltpu.VMEM((D, 512), F32),
            pltpu.VMEM((4, C, 128), F32),
            pltpu.VMEM((4, C, 128), F32),
            dma((4,)),
            dma((10,)),
            dma((27,)),
            dma((8, 2)),
            dma((8,)),
            dma((8,)),
            dma((4, 2)),
            dma((4, 2)),
            dma((2,)),
            dma((2,)),
            dma((2, 4)),
            dma((2, 4)),
        ],
        compiler_params=pltpu.CompilerParams(
            vmem_limit_bytes=62 * 1024 * 1024, has_side_effects=True, collective_id=0
        ),
        name="denoise",
    )(
        latents, step_index, position, text, jnp.swapaxes(modulation, 0, 1), levels[None, :],
        q_gain[None, :], k_gain[None, :], embed_weight, final_weight.T, new_noise, qkv_weight, out_weight,
    )
    return both[1], both[0]


def solution(mesh):
    in_specs = (
        P("queue", None, "seq"), P("queue"), P(), P(), P(), P("seq", None), P(), P(), P(),
        P(None, None, "seq"), P(), P(), P(None, "seq"),
    )
    out_specs = (P("queue", None, "seq"), P("queue", None, "seq"))
    return jax.shard_map(body, mesh=mesh, in_specs=in_specs, out_specs=out_specs, check_vma=False)
```

```python
import functools
import math

import jax
import jax.numpy as jnp
from jax import lax
from jax.experimental import pallas as pl
from jax.experimental.pallas import tpu as pltpu
from jax.sharding import PartitionSpec as P

F32, BF = jnp.float32, jnp.bfloat16
MESH = pl.DeviceIdType.MESH
EPS = 1e-6
D, H, HD, C, TXT, HP = 1152, 16, 72, 16, 128, 80
ROWS = TXT + 16
CUT = 64
PARTS = ((0, CUT), (CUT, ROWS - CUT))


def nn(a, b):
    return lax.dot_general(a, b, (((1,), (0,)), ((), ())), preferred_element_type=F32)


def nt(a, b):
    return lax.dot_general(a, b, (((1,), (1,)), ((), ())), preferred_element_type=F32)


def tn(a, b):
    return lax.dot_general(a, b, (((0,), (0,)), ((), ())), preferred_element_type=F32)


def split3(x):
    a = x.astype(BF)
    r = x - a.astype(F32)
    b = r.astype(BF)
    c = (r - b.astype(F32)).astype(BF)
    return jnp.concatenate([a, b, c], axis=0)


def head_norm(rows, gain):
    ss = jnp.sum(rows * rows, axis=0, keepdims=True) * (1.0 / HD)
    return rows * lax.rsqrt(ss + EPS) * gain


def kernel(
    latents, steps, posin, text, mod, levels, qg, kg, ew, fw, noise, wqkv_hbm, wo_hbm,
    out,
    pos, lat, latx, gains8, gains, wqkv, wo, wt, wot, e3, mods, modsT, x, kT, vT, q, p_even, p_odd, tk, tv, att, attb, hid, ubuf, vbuf,
    w_sem, own_sem, pos_send, pos_recv, lat_send, lat_recv, kv_send, kv_recv, tx_send, tx_recv,
    out_send, out_recv,
):
    qd, sq = lax.axis_index("queue"), lax.axis_index("seq")
    c = lax.rem(qd, 2)
    y = lax.rem(qd // 2, 4)
    z = (qd // 8) * 4 + sq // 4
    zl, xx = sq // 4, lax.rem(sq, 4)
    h = zl // 2
    rz = lax.rem(zl, 2)
    partner = (qd + 1 - 2 * c, sq)
    frame = sq // 2
    part = lax.rem(sq, 2)
    base = qd - c

    def at_z(step):
        zz = lax.rem(z + step + 8, 8)
        return ((zz // 4) * 8 + y * 2 + c, lax.rem(zz, 4) * 4 + xx)

    def at_x(step):
        return (qd, zl * 4 + lax.rem(xx + step + 4, 4))

    def weights(k):
        if k < 3:
            cols = pl.ds(k * D, D)
            return pltpu.make_async_copy(wqkv_hbm.at[:, cols], wqkv.at[:, cols], w_sem.at[k])
        return pltpu.make_async_copy(wo_hbm, wo, w_sem.at[3])

    for k in range(4):
        weights(k).start()

    barrier = pltpu.get_barrier_semaphore()

    def greet(target):
        pl.semaphore_signal(barrier, inc=1, device_id=target, device_id_type=MESH)

    for target in (at_x(1), at_x(-1), at_z(1), at_z(-1), partner):
        greet(target)
    for n in range(8):

        @pl.when(jnp.logical_or(base + h != qd, 8 * c + n != sq))
        def _(n=n):
            greet((base + h, 8 * c + n))

    after = (qd + 1) // 2 * 2

    @pl.when(qd < 15)
    def _():
        greet((after + h, 8 * lax.rem(qd + 1, 2) + lax.rem(sq, 8) // 4))

    starts = jnp.logical_or(sq // 2 == 4, jnp.logical_and(sq // 2 == 0, base > 0))
    with jax.named_scope("entry"):
        pl.semaphore_wait(barrier, 13 - jnp.where(c == h, 1, 0) + jnp.where(starts, 4, 0))

    def rows_of(ref, color):
        low, size = PARTS[color]
        return ref.at[pl.ds(low, size), :]

    def send_block(src, slot, color, target, number):
        return pltpu.make_async_remote_copy(
            src_ref=rows_of(src, color),
            dst_ref=rows_of(pos.at[slot], color),
            send_sem=pos_send.at[number],
            recv_sem=pos_recv.at[slot, color],
            device_id=target,
            device_id_type=MESH,
        )

    def block_wait(slot, color):
        dst = rows_of(pos.at[slot], color)
        pltpu.make_async_copy(dst, dst, pos_recv.at[slot, color]).wait()

    own_slot = rz * 4 + xx
    mine = c == h
    odd = lax.rem(xx, 2)

    def own_copies():
        made = [pltpu.make_async_copy(posin, pos.at[own_slot, pl.ds(0, TXT), :], own_sem.at[9])]
        for j in range(9):
            dst = pos.at[own_slot, pl.ds(TXT, 16), pl.ds(128 * j, 128)]
            made.append(pltpu.make_async_copy(text.at[j], dst, own_sem.at[j]))
        return made

    def first_sends(color):
        src = posin if color == 0 else pos.at[own_slot]
        targets = (at_x(1), at_x(-1), at_z(1), at_z(-1))
        return [send_block(src, own_slot, color, t, 4 * color + k) for k, t in enumerate(targets)]

    def row_relays(k):
        slot = rz * 4 + lax.rem(xx + k, 4)
        return [send_block(pos.at[slot], slot, 0, at_z(s), 8 + 2 * (k - 1) + n) for n, s in enumerate((1, -1))]

    def row_hop():
        step = 2 * odd - 1
        slot = rz * 4 + lax.rem(xx - step + 4, 4)
        return send_block(pos.at[slot], slot, 0, at_x(step), 14)

    def column_relays(r):
        slot = r * 4 + xx
        return [send_block(pos.at[slot], slot, 1, at_x(s), 15 + 2 * r + n) for n, s in enumerate((1, -1))]

    def delta(row):
        return lax.rem(2 * c + row - zl + 4, 4)

    def near(row):
        return lax.rem(delta(row), 2) == 1

    def z_hop(slot, color, row, number):
        return send_block(pos.at[slot], slot, color, at_z(delta(row) - 2), number)

    def column_hop_due(r):
        return jnp.logical_and(near(r), odd == jnp.where(delta(r) == 3, 0, 1))

    def row_hop_slot(r, k):
        return r * 4 + 2 * k + jnp.where(delta(r) == 3, 0, 1)

    def across_slot(r):
        return r * 4 + lax.rem(xx + (3, 1)[r], 4)

    def across_slot_of(row):
        return row * 4 + lax.rem(xx + 3 - 2 * row, 4)

    def across_hop(r):
        slot = across_slot(r)
        return send_block(pos.at[slot], slot, 1, at_x((1, -1)[r]), 25 + r)

    @pl.when(mine)
    def _():
        for copy in first_sends(0):
            copy.start()
        for copy in own_copies():
            copy.start()

    for n in range(4):
        latx[n, 0:C] = latents[n]
        latx[n, C:24] = jnp.full((8, 128), steps[n].astype(F32))
    fold = math.log2(math.e) / math.sqrt(HD)
    gains8[...] = jnp.zeros((8, 128), F32)
    gains8[0:1, 0:HD] = qg[...] * fold
    gains8[1:2, 0:HD] = kg[...]
    columns = gains8[...].T
    for k in range(2):
        gains[k] = jnp.broadcast_to(columns[0:HD, k : k + 1], (HD, 256))

    @pl.when(mine)
    def _():
        for copy in own_copies():
            copy.wait()
        for copy in first_sends(1):
            copy.start()

    lat_slot = lax.rem(sq, 8)

    def lat_target(n):
        return base + sq // 8, 8 * c + n

    def lat_copy(n):
        return pltpu.make_async_remote_copy(
            src_ref=latx.at[n // 2], dst_ref=lat.at[lat_slot], send_sem=lat_send.at[n],
            recv_sem=lat_recv.at[lat_slot], device_id=lat_target(n), device_id_type=MESH)

    def lat_local(n):
        return pltpu.make_async_copy(latx.at[n // 2], lat.at[lat_slot], lat_recv.at[lat_slot])

    for n in range(8):
        to_q, to_s = lat_target(n)
        away = jnp.logical_or(to_q != qd, to_s != sq)

        @pl.when(away)
        def _(n=n):
            lat_copy(n).start()

        @pl.when(jnp.logical_not(away))
        def _(n=n):
            lat_local(n).start()

    for j in range(3):
        e3[C * j : C * j + C, :] = ew[...]

    def turn(src, dst, first, count):
        def one(i, carry):
            o = pl.multiple_of(i * 128, 128)
            dst[pl.ds(o, 128), :] = src[:, pl.ds(o, 128)].T
            return carry

        lax.fori_loop(first, first + count, one, 0)

    with jax.named_scope("turnk"):
        weights(1).wait()
        turn(wqkv, wt, 9, 9)

    @pl.when(mine)
    def _():
        for k in (1, 3):
            block_wait(rz * 4 + lax.rem(xx + k, 4), 0)
        row_hop().start()
        for k in (1, 3):
            for copy in row_relays(k):
                copy.start()

    for r in range(2):

        @pl.when(near(r))
        def _(r=r):
            block_wait(r * 4 + xx, 1)

        @pl.when(column_hop_due(r))
        def _(r=r):
            z_hop(r * 4 + xx, 1, r, 19 + r).start()

        @pl.when(near(r))
        def _(r=r):
            for copy in column_relays(r):
                copy.start()

    with jax.named_scope("turnv"):
        weights(2).wait()
        turn(wqkv, wt, 18, 9)

    @pl.when(mine)
    def _():
        block_wait(rz * 4 + lax.rem(xx + 2, 4), 0)
        for copy in row_relays(2):
            copy.start()

    for r in range(2):

        @pl.when(delta(r) == 2)
        def _(r=r):
            block_wait(r * 4 + xx, 1)
            for copy in column_relays(r):
                copy.start()

    with jax.named_scope("latents"):
        for n in range(8):
            pltpu.make_async_copy(lat.at[n], lat.at[n], lat_recv.at[n]).wait()

    stepf = lat[0, 16:17, 0:1]
    plan = lax.broadcasted_iota(jnp.int32, mod.shape[1:], 0).astype(F32)
    for i in range(5):
        mods[i : i + 1, :] = jnp.sum(jnp.where(plan == stepf, mod[i], 0.0), axis=0, keepdims=True)
    mods[5:8, :] = jnp.zeros((3, D), F32)
    modsT[...] = mods[...].T
    lane = lax.broadcasted_iota(jnp.int32, levels.shape, 1).astype(F32)
    low = jnp.sum(jnp.where(lane == stepf, levels[...], 0.0), axis=1, keepdims=True)
    high = jnp.sum(jnp.where(lane == stepf + 1.0, levels[...], 0.0), axis=1, keepdims=True)
    step_size = high - low

    ones = (lax.broadcasted_iota(jnp.int32, (HP - HD, 256), 0) == 0).astype(F32)
    nothing = jnp.zeros((HP - HD, 256), F32)
    heads_at_once = 4
    rows_at_once = heads_at_once * HD

    def kv_copy(pair, which):
        ref = (kT, vT)[which]
        cols = pl.ds(pl.multiple_of(c * 1024 + pair * 256, 256), 256)
        return pltpu.make_async_remote_copy(
            src_ref=ref.at[:, :, cols], dst_ref=ref.at[:, :, cols], send_sem=kv_send.at[pair, which],
            recv_sem=kv_recv.at[pair, which], device_id=partner, device_id_type=MESH)

    def kv_wait(pair, which):
        ref = (kT, vT)[which]
        cols = pl.ds(pl.multiple_of((1 - c) * 1024 + pair * 256, 256), 256)
        dst = ref.at[:, :, cols]
        pltpu.make_async_copy(dst, dst, kv_recv.at[pair, which]).wait()

    def nth_row(n):
        return lax.rem(jnp.where(mine, rz, 1 - rz) + n // 2, 2)

    def nth_pair(n):
        return nth_row(n) * 2 + lax.rem(xx // 2 + n, 2)

    def later_hops():
        first = nth_pair(0)
        for r in range(2):

            @pl.when(near(r))
            def _(r=r):
                for k in range(2):
                    slot = row_hop_slot(r, k)

                    @pl.when(slot // 2 != first)
                    def _(slot=slot):
                        block_wait(slot, 0)

                    z_hop(slot, 0, r, 21 + 2 * r + k).start()

        for r in range(2):

            @pl.when(across_slot(r) // 2 != first)
            def _(r=r):
                block_wait(across_slot(r), 1)

            across_hop(r).start()

    def one_pair(n, carry):
        row = nth_row(n)
        pair = nth_pair(n)
        for k in range(2):
            slot = pair * 2 + k
            column = lax.rem(slot, 4)

            passed = jnp.where(delta(row) == 3, 0, jnp.where(delta(row) == 1, 1, 2))

            @pl.when(jnp.logical_and(delta(row) > 0, jnp.logical_or(n == 0, lax.rem(slot, 2) != passed)))
            def _(slot=slot):
                block_wait(slot, 0)

            @pl.when(jnp.logical_and(column != xx, jnp.logical_or(n == 0, slot != across_slot_of(row))))
            def _(slot=slot):
                block_wait(slot, 1)

        a, b = pair * 2, pair * 2 + 1
        l3 = jnp.concatenate([split3(lat[a, 0:C]), split3(lat[b, 0:C])], axis=1)
        places = jnp.concatenate([pos[a, 0:TXT], pos[b, 0:TXT]], axis=0)
        hidden = tn(l3, e3[...]) + places.astype(F32)
        center = hidden - jnp.mean(hidden, axis=-1, keepdims=True)
        unit = center * lax.rsqrt(jnp.mean(center * center, axis=-1, keepdims=True) + EPS)
        xb = (unit * (1.0 + mods[1:2]) + mods[0:1]).astype(BF)
        x[pair] = xb
        cols = pl.ds(pl.multiple_of(c * 1024 + pair * 256, 256), 256)
        for g in range(H // heads_at_once):
            o = D + g * rows_at_once
            r = nt(wt[o : o + rows_at_once, :], xb)
            for j in range(heads_at_once):
                rows = r[j * HD : (j + 1) * HD].astype(BF).astype(F32)
                padded = jnp.concatenate([head_norm(rows, gains[1]), nothing], axis=0)
                kT[g * heads_at_once + j, :, cols] = padded.astype(BF)
        for g in range(H // heads_at_once):
            o = 2 * D + g * rows_at_once
            r = nt(wt[o : o + rows_at_once, :], xb)
            for j in range(heads_at_once):
                padded = jnp.concatenate([r[j * HD : (j + 1) * HD], ones], axis=0)
                vT[g * heads_at_once + j, :, cols] = padded.astype(BF)
            if g == 0:
                kv_copy(pair, 0).start()
        for k in range(2):
            slot = pair * 2 + k
            t = jnp.concatenate([pos[slot, TXT:ROWS, 128 * j : 128 * j + 128] for j in range(9)], axis=0)
            t = t.astype(F32)
            keys = jnp.concatenate([head_norm(t[0:HD], gains[1, :, 0:128]), nothing[:, 0:128]], axis=0)
            tk[8 * c + slot] = keys.astype(BF)
            tv[8 * c + slot] = jnp.concatenate([t[HD : 2 * HD], ones[:, 0:128]], axis=0).astype(BF)

        kv_copy(pair, 1).start()

        @pl.when(n == 0)
        def _():
            later_hops()
            weights(0).wait()
            turn(wqkv, wt, 0, 9)

        @pl.when(n == 1)
        def _():
            weights(3).wait()
            turn(wo, wot, 0, 9)

        return carry

    with jax.named_scope("pairs"):
        lax.fori_loop(0, 4, one_pair, 0)

    def one_query_block(n, carry):
        xb = x[part * 2 + n]
        cols = pl.ds(pl.multiple_of(n * 256, 256), 256)
        for g in range(H // heads_at_once):
            o = g * rows_at_once
            r = nt(wt[o : o + rows_at_once, :], xb)
            for j in range(heads_at_once):
                rows = r[j * HD : (j + 1) * HD].astype(BF).astype(F32)
                padded = jnp.concatenate([head_norm(rows, gains[0]), jnp.zeros((128 - HD, 256), F32)], axis=0)
                q[g * heads_at_once + j, cols, :] = padded.T.astype(BF)

        return carry

    def tx_copy(which):
        ref = (tk, tv)[which]
        rows = pl.ds(8 * c, 8)
        return pltpu.make_async_remote_copy(
            src_ref=ref.at[rows], dst_ref=ref.at[rows], send_sem=tx_send.at[which],
            recv_sem=tx_recv.at[which], device_id=partner, device_id_type=MESH)

    def tx_wait(which):
        dst = (tk, tv)[which].at[pl.ds(8 * (1 - c), 8)]
        pltpu.make_async_copy(dst, dst, tx_recv.at[which]).wait()

    for which in range(2):
        tx_copy(which).start()
    with jax.named_scope("queries"):
        lax.fori_loop(0, 2, one_query_block, 0)
    with jax.named_scope("partner"):
        for which in range(2):
            tx_wait(which)
            for pair in range(4):
                kv_wait(pair, which)

    def scores(n, keys, dst, rows, cols):
        dst[rows, cols] = jnp.exp2(nn(q[n, rows, 0:HP], keys)).astype(BF)

    halves = (slice(0, 256), slice(256, 512))
    own_cols = [slice(256 * k, 256 * k + 256) for k in range(8)]
    text_cols = slice(2048, 2048 + TXT)

    def stage(ahead, dst, behind, src):
        made = [None, None]
        for cols in own_cols:
            for k, rows in enumerate(halves):
                if ahead is not None:
                    scores(ahead, kT[ahead, :, cols], dst, rows, cols)
                if behind is not None:
                    term = nt(vT[behind, :, cols], src[rows, cols])
                    made[k] = term if made[k] is None else made[k] + term
        if ahead is not None:
            scores(ahead, tk[ahead], dst, slice(0, 512), text_cols)
        if behind is not None:
            own = jnp.concatenate(made, axis=1)
            text = nt(tv[behind], src[:, text_cols])
            total = own[0:HD] / own[HD : HD + 1] + text[0:HD] / text[HD : HD + 1]
            att[pl.ds(pl.multiple_of(behind * HD, 8), HD), :] = total

    def two_heads(n, carry):
        stage(2 * n + 1, p_odd, 2 * n, p_even)
        stage(2 * n + 2, p_even, 2 * n + 1, p_odd)
        return carry

    with jax.named_scope("attention"):
        stage(0, p_even, None, None)
        lax.fori_loop(0, H // 2 - 1, two_heads, 0)
        stage(H - 1, p_odd, H - 2, p_even)
        stage(None, None, H - 1, p_odd)

    attb[...] = att[...].astype(BF)
    for t in range(4):
        slot = part * 4 + t
        hid[:, t * 128 : t * 128 + 128] = tn(e3[...], split3(lat[slot, 0:C])) + pos[slot, 0:TXT].T.astype(F32)
    for g in range(2):
        r = slice(g * 576, g * 576 + 576)
        hid[r, :] = hid[r, :] + modsT[r, 2:3] * nn(wot[r, :], attb[...])
    hidden = hid[...]
    center = hidden - jnp.sum(hidden, axis=0, keepdims=True) * (1.0 / D)
    scale = lax.rsqrt(jnp.sum(center * center, axis=0, keepdims=True) * (1.0 / D) + EPS)
    xb = (center * scale * (1.0 + modsT[:, 4:5]) + modsT[:, 3:4]).astype(BF)
    speed = nn(fw[...], xb)
    for t in range(4):
        piece = speed[:, t * 128 : t * 128 + 128]
        vbuf[t] = piece
        ubuf[t] = lat[part * 4 + t, 0:C] + step_size * piece

    whole = (qd // 2) * 8 + frame
    before = jnp.maximum(whole - 1, 0)

    def out_copy(which, t):
        src, dst, place = ((vbuf, 0, whole), (ubuf, 1, before))[which]
        there = lax.rem(place, 4)
        return pltpu.make_async_remote_copy(
            src_ref=src.at[t], dst_ref=out.at[dst, there], send_sem=out_send.at[which, t],
            recv_sem=out_recv.at[which, there],
            device_id=(place // 4, 8 * c + 4 * part + t), device_id_type=MESH)

    def out_local(which, t):
        src, dst, place = ((vbuf, 0, whole), (ubuf, 1, before))[which]
        there = lax.rem(place, 4)
        return pltpu.make_async_copy(src.at[t], out.at[dst, there], out_recv.at[which, there])

    def out_cases(which, t):
        place = (whole, before)[which]
        here = jnp.logical_and(place // 4 == qd, 8 * c + 4 * part + t == sq)
        away = jnp.logical_not(here)
        if which == 1:
            here = jnp.logical_and(here, whole > 0)
            away = jnp.logical_and(away, whole > 0)
        return here, away

    for which in range(2):
        for t in range(4):
            here, away = out_cases(which, t)

            @pl.when(away)
            def _(which=which, t=t):
                out_copy(which, t).start()

            @pl.when(here)
            def _(which=which, t=t):
                out_local(which, t).start()

    @pl.when(mine)
    def _():
        for color in range(2):
            for copy in first_sends(color):
                copy.wait_send()
        row_hop().wait_send()
        for k in range(1, 4):
            for copy in row_relays(k):
                copy.wait_send()

    for r in range(2):

        @pl.when(delta(r) > 0)
        def _(r=r):
            for copy in column_relays(r):
                copy.wait_send()

        @pl.when(column_hop_due(r))
        def _(r=r):
            z_hop(r * 4 + xx, 1, r, 19 + r).wait_send()

        @pl.when(near(r))
        def _(r=r):
            for k in range(2):
                z_hop(row_hop_slot(r, k), 0, r, 21 + 2 * r + k).wait_send()

        across_hop(r).wait_send()

    for n in range(8):
        to_q, to_s = lat_target(n)

        @pl.when(jnp.logical_or(to_q != qd, to_s != sq))
        def _(n=n):
            lat_copy(n).wait_send()

    for which in range(2):
        tx_copy(which).wait_send()
        for pair in range(4):
            kv_copy(pair, which).wait_send()
        for t in range(4):

            @pl.when(out_cases(which, t)[1])
            def _(which=which, t=t):
                out_copy(which, t).wait_send()

    with jax.named_scope("arrivals"):
        for which, count in ((0, 4), (1, 3)):
            for n in range(count):
                dst = out.at[which, n]
                pltpu.make_async_copy(dst, dst, out_recv.at[which, n]).wait()

    @pl.when(qd < 15)
    def _():
        dst = out.at[1, 3]
        pltpu.make_async_copy(dst, dst, out_recv.at[1, 3]).wait()

    @pl.when(qd == 15)
    def _():
        out[1, 3] = noise[...]


def body(
    latents, step_index, levels, modulation, embed_weight, position, qkv_weight, q_gain, k_gain,
    text_kv, out_weight, final_weight, new_noise,
):
    text = jnp.swapaxes(text_kv, 1, 2).reshape(9, 16, TXT)
    inner = pl.BlockSpec(memory_space=pltpu.VMEM)
    outer = pl.BlockSpec(memory_space=pl.ANY)
    dma = pltpu.SemaphoreType.DMA
    scalars = pl.BlockSpec(memory_space=pltpu.SMEM)
    both = pl.pallas_call(
        kernel,
        out_shape=jax.ShapeDtypeStruct((2,) + latents.shape, F32),
        in_specs=[inner, scalars] + [inner] * 9 + [outer] * 2,
        out_specs=inner,
        scratch_shapes=[
            pltpu.VMEM((8, ROWS, D), BF),
            pltpu.VMEM((8, 24, 128), F32),
            pltpu.VMEM((4, 24, 128), F32),
            pltpu.VMEM((8, 128), F32),
            pltpu.VMEM((2, HD, 256), F32),
            pltpu.VMEM((D, 3 * D), BF),
            pltpu.VMEM((D, D), BF),
            pltpu.VMEM((3 * D, D), BF),
            pltpu.VMEM((D, D), BF),
            pltpu.VMEM((3 * C, D), BF),
            pltpu.VMEM((8, D), F32),
            pltpu.VMEM((D, 8), F32),
            pltpu.VMEM((4, 256, D), BF),
            pltpu.VMEM((H, HP, 2048), BF),
            pltpu.VMEM((H, HP, 2048), BF),
            pltpu.VMEM((H, 512, 128), BF),
            pltpu.VMEM((512, 2048 + TXT), BF),
            pltpu.VMEM((512, 2048 + TXT), BF),
            pltpu.VMEM((H, HP, TXT), BF),
            pltpu.VMEM((H, HP, TXT), BF),
            pltpu.VMEM((D, 512), F32),
            pltpu.VMEM((D, 512), BF),
            pltpu.VMEM((D, 512), F32),
            pltpu.VMEM((4, C, 128), F32),
            pltpu.VMEM((4, C, 128), F32),
            dma((4,)),
            dma((10,)),
            dma((27,)),
            dma((8, 2)),
            dma((8,)),
            dma((8,)),
            dma((4, 2)),
            dma((4, 2)),
            dma((2,)),
            dma((2,)),
            dma((2, 4)),
            dma((2, 4)),
        ],
        compiler_params=pltpu.CompilerParams(
            vmem_limit_bytes=62 * 1024 * 1024, has_side_effects=True, collective_id=0
        ),
        name="denoise",
    )(
        latents, step_index, position, text, jnp.swapaxes(modulation, 0, 1), levels[None, :],
        q_gain[None, :], k_gain[None, :], embed_weight, final_weight.T, new_noise, qkv_weight, out_weight,
    )
    return both[1], both[0]


def solution(mesh):
    in_specs = (
        P("queue", None, "seq"), P("queue"), P(), P(), P(), P("seq", None), P(), P(), P(),
        P(None, None, "seq"), P(), P(), P(None, "seq"),
    )
    out_specs = (P("queue", None, "seq"), P("queue", None, "seq"))
    return jax.shard_map(body, mesh=mesh, in_specs=in_specs, out_specs=out_specs, check_vma=False)
```

```python
import functools
import math

import jax
import jax.numpy as jnp
from jax import lax
from jax.experimental import pallas as pl
from jax.experimental.pallas import tpu as pltpu
from jax.sharding import PartitionSpec as P

F32, BF = jnp.float32, jnp.bfloat16
MESH = pl.DeviceIdType.MESH
EPS = 1e-6
D, H, HD, C, TXT, HP = 1152, 16, 72, 16, 128, 80
ROWS = TXT + 16
CUT = 64
PARTS = ((0, CUT), (CUT, ROWS - CUT))


def nn(a, b):
    return lax.dot_general(a, b, (((1,), (0,)), ((), ())), preferred_element_type=F32)


def nt(a, b):
    return lax.dot_general(a, b, (((1,), (1,)), ((), ())), preferred_element_type=F32)


def tn(a, b):
    return lax.dot_general(a, b, (((0,), (0,)), ((), ())), preferred_element_type=F32)


def split3(x):
    a = x.astype(BF)
    r = x - a.astype(F32)
    b = r.astype(BF)
    c = (r - b.astype(F32)).astype(BF)
    return jnp.concatenate([a, b, c], axis=0)


def head_norm(rows, gain):
    ss = jnp.sum(rows * rows, axis=0, keepdims=True) * (1.0 / HD)
    return rows * lax.rsqrt(ss + EPS) * gain


def kernel(
    latents, steps, posin, text, mod, levels, qg, kg, ew, fw, noise, wqkv_hbm, wo_hbm,
    out,
    pos, lat, latx, gains8, gains, wqkv, wo, wt, wot, e3, mods, modsT, x, kT, vT, q, p_even, p_odd, tk, tv, att, attb, hid, ubuf, vbuf,
    w_sem, own_sem, pos_send, pos_recv, lat_send, lat_recv, kv_send, kv_recv, tx_send, tx_recv,
    out_send, out_recv,
):
    qd, sq = lax.axis_index("queue"), lax.axis_index("seq")
    c = lax.rem(qd, 2)
    y = lax.rem(qd // 2, 4)
    z = (qd // 8) * 4 + sq // 4
    zl, xx = sq // 4, lax.rem(sq, 4)
    h = zl // 2
    rz = lax.rem(zl, 2)
    partner = (qd + 1 - 2 * c, sq)
    frame = sq // 2
    part = lax.rem(sq, 2)
    base = qd - c

    def at_z(step):
        zz = lax.rem(z + step + 8, 8)
        return ((zz // 4) * 8 + y * 2 + c, lax.rem(zz, 4) * 4 + xx)

    def at_x(step):
        return (qd, zl * 4 + lax.rem(xx + step + 4, 4))

    def weights(k):
        if k < 3:
            cols = pl.ds(k * D, D)
            return pltpu.make_async_copy(wqkv_hbm.at[:, cols], wqkv.at[:, cols], w_sem.at[k])
        return pltpu.make_async_copy(wo_hbm, wo, w_sem.at[3])

    for k in range(4):
        weights(k).start()

    barrier = pltpu.get_barrier_semaphore()

    def greet(target):
        pl.semaphore_signal(barrier, inc=1, device_id=target, device_id_type=MESH)

    for target in (at_x(1), at_x(-1), at_z(1), at_z(-1), partner):
        greet(target)
    for n in range(8):

        @pl.when(jnp.logical_or(base + h != qd, 8 * c + n != sq))
        def _(n=n):
            greet((base + h, 8 * c + n))

    after = (qd + 1) // 2 * 2

    @pl.when(qd < 15)
    def _():
        greet((after + h, 8 * lax.rem(qd + 1, 2) + lax.rem(sq, 8) // 4))

    starts = jnp.logical_or(sq // 2 == 4, jnp.logical_and(sq // 2 == 0, base > 0))
    with jax.named_scope("entry"):
        pl.semaphore_wait(barrier, 13 - jnp.where(c == h, 1, 0) + jnp.where(starts, 4, 0))

    def rows_of(ref, color):
        low, size = PARTS[color]
        return ref.at[pl.ds(low, size), :]

    def send_block(src, slot, color, target, number):
        return pltpu.make_async_remote_copy(
            src_ref=rows_of(src, color),
            dst_ref=rows_of(pos.at[slot], color),
            send_sem=pos_send.at[number],
            recv_sem=pos_recv.at[slot, color],
            device_id=target,
            device_id_type=MESH,
        )

    def block_wait(slot, color):
        dst = rows_of(pos.at[slot], color)
        pltpu.make_async_copy(dst, dst, pos_recv.at[slot, color]).wait()

    own_slot = rz * 4 + xx
    mine = c == h
    odd = lax.rem(xx, 2)

    def own_copies():
        made = [pltpu.make_async_copy(posin, pos.at[own_slot, pl.ds(0, TXT), :], own_sem.at[9])]
        for j in range(9):
            dst = pos.at[own_slot, pl.ds(TXT, 16), pl.ds(128 * j, 128)]
            made.append(pltpu.make_async_copy(text.at[j], dst, own_sem.at[j]))
        return made

    def first_sends(color):
        src = posin if color == 0 else pos.at[own_slot]
        targets = (at_x(1), at_x(-1), at_z(1), at_z(-1))
        return [send_block(src, own_slot, color, t, 4 * color + k) for k, t in enumerate(targets)]

    def row_relays(k):
        slot = rz * 4 + lax.rem(xx + k, 4)
        return [send_block(pos.at[slot], slot, 0, at_z(s), 8 + 2 * (k - 1) + n) for n, s in enumerate((1, -1))]

    def row_hop():
        step = 2 * odd - 1
        slot = rz * 4 + lax.rem(xx - step + 4, 4)
        return send_block(pos.at[slot], slot, 0, at_x(step), 14)

    def column_relays(r):
        slot = r * 4 + xx
        return [send_block(pos.at[slot], slot, 1, at_x(s), 15 + 2 * r + n) for n, s in enumerate((1, -1))]

    def delta(row):
        return lax.rem(2 * c + row - zl + 4, 4)

    def near(row):
        return lax.rem(delta(row), 2) == 1

    def z_hop(slot, color, row, number):
        return send_block(pos.at[slot], slot, color, at_z(delta(row) - 2), number)

    def column_hop_due(r):
        return jnp.logical_and(near(r), odd == jnp.where(delta(r) == 3, 0, 1))

    def row_hop_slot(r, k):
        return r * 4 + 2 * k + jnp.where(delta(r) == 3, 0, 1)

    def across_slot(r):
        return r * 4 + lax.rem(xx + (3, 1)[r], 4)

    def across_slot_of(row):
        return row * 4 + lax.rem(xx + 3 - 2 * row, 4)

    def across_hop(r):
        slot = across_slot(r)
        return send_block(pos.at[slot], slot, 1, at_x((1, -1)[r]), 25 + r)

    @pl.when(mine)
    def _():
        for copy in first_sends(0):
            copy.start()
        for copy in own_copies():
            copy.start()

    for n in range(4):
        latx[n, 0:C] = latents[n]
        latx[n, C:24] = jnp.full((8, 128), steps[n].astype(F32))
    fold = math.log2(math.e) / math.sqrt(HD)
    gains8[...] = jnp.zeros((8, 128), F32)
    gains8[0:1, 0:HD] = qg[...] * fold
    gains8[1:2, 0:HD] = kg[...]
    columns = gains8[...].T
    for k in range(2):
        gains[k] = jnp.broadcast_to(columns[0:HD, k : k + 1], (HD, 256))

    @pl.when(mine)
    def _():
        for copy in own_copies():
            copy.wait()
        for copy in first_sends(1):
            copy.start()

    lat_slot = lax.rem(sq, 8)

    def lat_target(n):
        return base + sq // 8, 8 * c + n

    def lat_copy(n):
        return pltpu.make_async_remote_copy(
            src_ref=latx.at[n // 2], dst_ref=lat.at[lat_slot], send_sem=lat_send.at[n],
            recv_sem=lat_recv.at[lat_slot], device_id=lat_target(n), device_id_type=MESH)

    def lat_local(n):
        return pltpu.make_async_copy(latx.at[n // 2], lat.at[lat_slot], lat_recv.at[lat_slot])

    for n in range(8):
        to_q, to_s = lat_target(n)
        away = jnp.logical_or(to_q != qd, to_s != sq)

        @pl.when(away)
        def _(n=n):
            lat_copy(n).start()

        @pl.when(jnp.logical_not(away))
        def _(n=n):
            lat_local(n).start()

    for j in range(3):
        e3[C * j : C * j + C, :] = ew[...]

    def turn(src, dst, first, count):
        def one(i, carry):
            o = pl.multiple_of(i * 128, 128)
            dst[pl.ds(o, 128), :] = src[:, pl.ds(o, 128)].T
            return carry

        lax.fori_loop(first, first + count, one, 0)

    with jax.named_scope("turnk"):
        weights(1).wait()
        turn(wqkv, wt, 9, 9)

    @pl.when(mine)
    def _():
        for k in (1, 3):
            block_wait(rz * 4 + lax.rem(xx + k, 4), 0)
        row_hop().start()
        for k in (1, 3):
            for copy in row_relays(k):
                copy.start()

    for r in range(2):

        @pl.when(near(r))
        def _(r=r):
            block_wait(r * 4 + xx, 1)

        @pl.when(column_hop_due(r))
        def _(r=r):
            z_hop(r * 4 + xx, 1, r, 19 + r).start()

        @pl.when(near(r))
        def _(r=r):
            for copy in column_relays(r):
                copy.start()

    with jax.named_scope("turnv"):
        weights(2).wait()
        turn(wqkv, wt, 18, 9)

    @pl.when(mine)
    def _():
        block_wait(rz * 4 + lax.rem(xx + 2, 4), 0)
        for copy in row_relays(2):
            copy.start()

    for r in range(2):

        @pl.when(delta(r) == 2)
        def _(r=r):
            block_wait(r * 4 + xx, 1)
            for copy in column_relays(r):
                copy.start()

    with jax.named_scope("latents"):
        for n in range(8):
            pltpu.make_async_copy(lat.at[n], lat.at[n], lat_recv.at[n]).wait()

    stepf = lat[0, 16:17, 0:1]
    plan = lax.broadcasted_iota(jnp.int32, mod.shape[1:], 0).astype(F32)
    for i in range(5):
        mods[i : i + 1, :] = jnp.sum(jnp.where(plan == stepf, mod[i], 0.0), axis=0, keepdims=True)
    mods[5:8, :] = jnp.zeros((3, D), F32)
    modsT[...] = mods[...].T
    lane = lax.broadcasted_iota(jnp.int32, levels.shape, 1).astype(F32)
    low = jnp.sum(jnp.where(lane == stepf, levels[...], 0.0), axis=1, keepdims=True)
    high = jnp.sum(jnp.where(lane == stepf + 1.0, levels[...], 0.0), axis=1, keepdims=True)
    step_size = high - low

    ones = (lax.broadcasted_iota(jnp.int32, (HP - HD, 256), 0) == 0).astype(F32)
    nothing = jnp.zeros((HP - HD, 256), F32)
    heads_at_once = 4
    rows_at_once = heads_at_once * HD

    def kv_copy(pair, which):
        ref = (kT, vT)[which]
        cols = pl.ds(pl.multiple_of(c * 1024 + pair * 256, 256), 256)
        return pltpu.make_async_remote_copy(
            src_ref=ref.at[:, :, cols], dst_ref=ref.at[:, :, cols], send_sem=kv_send.at[pair, which],
            recv_sem=kv_recv.at[pair, which], device_id=partner, device_id_type=MESH)

    def kv_wait(pair, which):
        ref = (kT, vT)[which]
        cols = pl.ds(pl.multiple_of((1 - c) * 1024 + pair * 256, 256), 256)
        dst = ref.at[:, :, cols]
        pltpu.make_async_copy(dst, dst, kv_recv.at[pair, which]).wait()

    def nth_row(n):
        return lax.rem(jnp.where(mine, rz, 1 - rz) + n // 2, 2)

    def nth_pair(n):
        return nth_row(n) * 2 + lax.rem(xx // 2 + n, 2)

    def later_hops():
        first = nth_pair(0)
        for r in range(2):

            @pl.when(near(r))
            def _(r=r):
                for k in range(2):
                    slot = row_hop_slot(r, k)

                    @pl.when(slot // 2 != first)
                    def _(slot=slot):
                        block_wait(slot, 0)

                    z_hop(slot, 0, r, 21 + 2 * r + k).start()

        for r in range(2):

            @pl.when(across_slot(r) // 2 != first)
            def _(r=r):
                block_wait(across_slot(r), 1)

            across_hop(r).start()

    def one_pair(n, carry):
        row = nth_row(n)
        pair = nth_pair(n)
        for k in range(2):
            slot = pair * 2 + k
            column = lax.rem(slot, 4)

            passed = jnp.where(delta(row) == 3, 0, jnp.where(delta(row) == 1, 1, 2))

            @pl.when(jnp.logical_and(delta(row) > 0, jnp.logical_or(n == 0, lax.rem(slot, 2) != passed)))
            def _(slot=slot):
                block_wait(slot, 0)

            @pl.when(jnp.logical_and(column != xx, jnp.logical_or(n == 0, slot != across_slot_of(row))))
            def _(slot=slot):
                block_wait(slot, 1)

        a, b = pair * 2, pair * 2 + 1
        l3 = jnp.concatenate([split3(lat[a, 0:C]), split3(lat[b, 0:C])], axis=1)
        places = jnp.concatenate([pos[a, 0:TXT], pos[b, 0:TXT]], axis=0)
        hidden = tn(l3, e3[...]) + places.astype(F32)
        center = hidden - jnp.mean(hidden, axis=-1, keepdims=True)
        unit = center * lax.rsqrt(jnp.mean(center * center, axis=-1, keepdims=True) + EPS)
        xb = (unit * (1.0 + mods[1:2]) + mods[0:1]).astype(BF)
        x[pair] = xb
        cols = pl.ds(pl.multiple_of(c * 1024 + pair * 256, 256), 256)
        for g in range(H // heads_at_once):
            o = D + g * rows_at_once
            r = nt(wt[o : o + rows_at_once, :], xb)
            for j in range(heads_at_once):
                rows = r[j * HD : (j + 1) * HD].astype(BF).astype(F32)
                padded = jnp.concatenate([head_norm(rows, gains[1]), nothing], axis=0)
                kT[g * heads_at_once + j, :, cols] = padded.astype(BF)
        for g in range(H // heads_at_once):
            o = 2 * D + g * rows_at_once
            r = nt(wt[o : o + rows_at_once, :], xb)
            for j in range(heads_at_once):
                padded = jnp.concatenate([r[j * HD : (j + 1) * HD], ones], axis=0)
                vT[g * heads_at_once + j, :, cols] = padded.astype(BF)
            if g == 0:
                kv_copy(pair, 0).start()
        for k in range(2):
            slot = pair * 2 + k
            t = jnp.concatenate([pos[slot, TXT:ROWS, 128 * j : 128 * j + 128] for j in range(9)], axis=0)
            t = t.astype(F32)
            keys = jnp.concatenate([head_norm(t[0:HD], gains[1, :, 0:128]), nothing[:, 0:128]], axis=0)
            tk[8 * c + slot] = keys.astype(BF)
            tv[8 * c + slot] = jnp.concatenate([t[HD : 2 * HD], ones[:, 0:128]], axis=0).astype(BF)

        kv_copy(pair, 1).start()

        @pl.when(n == 0)
        def _():
            later_hops()
            weights(0).wait()
            turn(wqkv, wt, 0, 9)

        @pl.when(row == part)
        def _():
            for k in range(2):
                slot = pair * 2 + k
                cols = pl.ds(pl.multiple_of((lax.rem(pair, 2) * 2 + k) * 128, 128), 128)
                places = pos[slot, 0:TXT].T.astype(F32)
                hid[:, cols] = tn(e3[...], split3(lat[slot, 0:C])) + places

        @pl.when(n == 1)
        def _():
            weights(3).wait()
            turn(wo, wot, 0, 9)

        return carry

    with jax.named_scope("pairs"):
        lax.fori_loop(0, 4, one_pair, 0)

    def one_query_block(n, carry):
        xb = x[part * 2 + n]
        cols = pl.ds(pl.multiple_of(n * 256, 256), 256)
        for g in range(H // heads_at_once):
            o = g * rows_at_once
            r = nt(wt[o : o + rows_at_once, :], xb)
            for j in range(heads_at_once):
                rows = r[j * HD : (j + 1) * HD].astype(BF).astype(F32)
                padded = jnp.concatenate([head_norm(rows, gains[0]), jnp.zeros((128 - HD, 256), F32)], axis=0)
                q[g * heads_at_once + j, cols, :] = padded.T.astype(BF)

        return carry

    def tx_copy(which):
        ref = (tk, tv)[which]
        rows = pl.ds(8 * c, 8)
        return pltpu.make_async_remote_copy(
            src_ref=ref.at[rows], dst_ref=ref.at[rows], send_sem=tx_send.at[which],
            recv_sem=tx_recv.at[which], device_id=partner, device_id_type=MESH)

    def tx_wait(which):
        dst = (tk, tv)[which].at[pl.ds(8 * (1 - c), 8)]
        pltpu.make_async_copy(dst, dst, tx_recv.at[which]).wait()

    for which in range(2):
        tx_copy(which).start()
    with jax.named_scope("queries"):
        lax.fori_loop(0, 2, one_query_block, 0)
    with jax.named_scope("partner"):
        for which in range(2):
            tx_wait(which)
            for pair in range(4):
                kv_wait(pair, which)

    def scores(n, keys, dst, rows, cols):
        dst[rows, cols] = jnp.exp2(nn(q[n, rows, 0:HP], keys)).astype(BF)

    halves = (slice(0, 256), slice(256, 512))
    own_cols = [slice(256 * k, 256 * k + 256) for k in range(8)]
    text_cols = slice(2048, 2048 + TXT)

    def stage(ahead, dst, behind, src):
        made = [None, None]
        for cols in own_cols:
            for k, rows in enumerate(halves):
                if ahead is not None:
                    scores(ahead, kT[ahead, :, cols], dst, rows, cols)
                if behind is not None:
                    term = nt(vT[behind, :, cols], src[rows, cols])
                    made[k] = term if made[k] is None else made[k] + term
        if ahead is not None:
            scores(ahead, tk[ahead], dst, slice(0, 512), text_cols)
        if behind is not None:
            own = jnp.concatenate(made, axis=1)
            text = nt(tv[behind], src[:, text_cols])
            total = own[0:HD] / own[HD : HD + 1] + text[0:HD] / text[HD : HD + 1]
            att[pl.ds(pl.multiple_of(behind * HD, 8), HD), :] = total

    def two_heads(n, carry):
        stage(2 * n + 1, p_odd, 2 * n, p_even)
        stage(2 * n + 2, p_even, 2 * n + 1, p_odd)
        return carry

    with jax.named_scope("attention"):
        stage(0, p_even, None, None)
        lax.fori_loop(0, H // 2 - 1, two_heads, 0)
        stage(H - 1, p_odd, H - 2, p_even)
        stage(None, None, H - 1, p_odd)

    attb[...] = att[...].astype(BF)
    for g in range(2):
        r = slice(g * 576, g * 576 + 576)
        hid[r, :] = hid[r, :] + modsT[r, 2:3] * nn(wot[r, :], attb[...])
    hidden = hid[...]
    center = hidden - jnp.sum(hidden, axis=0, keepdims=True) * (1.0 / D)
    scale = lax.rsqrt(jnp.sum(center * center, axis=0, keepdims=True) * (1.0 / D) + EPS)
    xb = (center * scale * (1.0 + modsT[:, 4:5]) + modsT[:, 3:4]).astype(BF)
    speed = nn(fw[...], xb)
    for t in range(4):
        piece = speed[:, t * 128 : t * 128 + 128]
        vbuf[t] = piece
        ubuf[t] = lat[part * 4 + t, 0:C] + step_size * piece

    whole = (qd // 2) * 8 + frame
    before = jnp.maximum(whole - 1, 0)

    def out_copy(which, t):
        src, dst, place = ((vbuf, 0, whole), (ubuf, 1, before))[which]
        there = lax.rem(place, 4)
        return pltpu.make_async_remote_copy(
            src_ref=src.at[t], dst_ref=out.at[dst, there], send_sem=out_send.at[which, t],
            recv_sem=out_recv.at[which, there],
            device_id=(place // 4, 8 * c + 4 * part + t), device_id_type=MESH)

    def out_local(which, t):
        src, dst, place = ((vbuf, 0, whole), (ubuf, 1, before))[which]
        there = lax.rem(place, 4)
        return pltpu.make_async_copy(src.at[t], out.at[dst, there], out_recv.at[which, there])

    def out_cases(which, t):
        place = (whole, before)[which]
        here = jnp.logical_and(place // 4 == qd, 8 * c + 4 * part + t == sq)
        away = jnp.logical_not(here)
        if which == 1:
            here = jnp.logical_and(here, whole > 0)
            away = jnp.logical_and(away, whole > 0)
        return here, away

    for which in range(2):
        for t in range(4):
            here, away = out_cases(which, t)

            @pl.when(away)
            def _(which=which, t=t):
                out_copy(which, t).start()

            @pl.when(here)
            def _(which=which, t=t):
                out_local(which, t).start()

    @pl.when(mine)
    def _():
        for color in range(2):
            for copy in first_sends(color):
                copy.wait_send()
        row_hop().wait_send()
        for k in range(1, 4):
            for copy in row_relays(k):
                copy.wait_send()

    for r in range(2):

        @pl.when(delta(r) > 0)
        def _(r=r):
            for copy in column_relays(r):
                copy.wait_send()

        @pl.when(column_hop_due(r))
        def _(r=r):
            z_hop(r * 4 + xx, 1, r, 19 + r).wait_send()

        @pl.when(near(r))
        def _(r=r):
            for k in range(2):
                z_hop(row_hop_slot(r, k), 0, r, 21 + 2 * r + k).wait_send()

        across_hop(r).wait_send()

    for n in range(8):
        to_q, to_s = lat_target(n)

        @pl.when(jnp.logical_or(to_q != qd, to_s != sq))
        def _(n=n):
            lat_copy(n).wait_send()

    for which in range(2):
        tx_copy(which).wait_send()
        for pair in range(4):
            kv_copy(pair, which).wait_send()
        for t in range(4):

            @pl.when(out_cases(which, t)[1])
            def _(which=which, t=t):
                out_copy(which, t).wait_send()

    with jax.named_scope("arrivals"):
        for which, count in ((0, 4), (1, 3)):
            for n in range(count):
                dst = out.at[which, n]
                pltpu.make_async_copy(dst, dst, out_recv.at[which, n]).wait()

    @pl.when(qd < 15)
    def _():
        dst = out.at[1, 3]
        pltpu.make_async_copy(dst, dst, out_recv.at[1, 3]).wait()

    @pl.when(qd == 15)
    def _():
        out[1, 3] = noise[...]


def body(
    latents, step_index, levels, modulation, embed_weight, position, qkv_weight, q_gain, k_gain,
    text_kv, out_weight, final_weight, new_noise,
):
    text = jnp.swapaxes(text_kv, 1, 2).reshape(9, 16, TXT)
    inner = pl.BlockSpec(memory_space=pltpu.VMEM)
    outer = pl.BlockSpec(memory_space=pl.ANY)
    dma = pltpu.SemaphoreType.DMA
    scalars = pl.BlockSpec(memory_space=pltpu.SMEM)
    both = pl.pallas_call(
        kernel,
        out_shape=jax.ShapeDtypeStruct((2,) + latents.shape, F32),
        in_specs=[inner, scalars] + [inner] * 9 + [outer] * 2,
        out_specs=inner,
        scratch_shapes=[
            pltpu.VMEM((8, ROWS, D), BF),
            pltpu.VMEM((8, 24, 128), F32),
            pltpu.VMEM((4, 24, 128), F32),
            pltpu.VMEM((8, 128), F32),
            pltpu.VMEM((2, HD, 256), F32),
            pltpu.VMEM((D, 3 * D), BF),
            pltpu.VMEM((D, D), BF),
            pltpu.VMEM((3 * D, D), BF),
            pltpu.VMEM((D, D), BF),
            pltpu.VMEM((3 * C, D), BF),
            pltpu.VMEM((8, D), F32),
            pltpu.VMEM((D, 8), F32),
            pltpu.VMEM((4, 256, D), BF),
            pltpu.VMEM((H, HP, 2048), BF),
            pltpu.VMEM((H, HP, 2048), BF),
            pltpu.VMEM((H, 512, 128), BF),
            pltpu.VMEM((512, 2048 + TXT), BF),
            pltpu.VMEM((512, 2048 + TXT), BF),
            pltpu.VMEM((H, HP, TXT), BF),
            pltpu.VMEM((H, HP, TXT), BF),
            pltpu.VMEM((D, 512), F32),
            pltpu.VMEM((D, 512), BF),
            pltpu.VMEM((D, 512), F32),
            pltpu.VMEM((4, C, 128), F32),
            pltpu.VMEM((4, C, 128), F32),
            dma((4,)),
            dma((10,)),
            dma((27,)),
            dma((8, 2)),
            dma((8,)),
            dma((8,)),
            dma((4, 2)),
            dma((4, 2)),
            dma((2,)),
            dma((2,)),
            dma((2, 4)),
            dma((2, 4)),
        ],
        compiler_params=pltpu.CompilerParams(
            vmem_limit_bytes=62 * 1024 * 1024, has_side_effects=True, collective_id=0
        ),
        name="denoise",
    )(
        latents, step_index, position, text, jnp.swapaxes(modulation, 0, 1), levels[None, :],
        q_gain[None, :], k_gain[None, :], embed_weight, final_weight.T, new_noise, qkv_weight, out_weight,
    )
    return both[1], both[0]


def solution(mesh):
    in_specs = (
        P("queue", None, "seq"), P("queue"), P(), P(), P(), P("seq", None), P(), P(), P(),
        P(None, None, "seq"), P(), P(), P(None, "seq"),
    )
    out_specs = (P("queue", None, "seq"), P("queue", None, "seq"))
    return jax.shard_map(body, mesh=mesh, in_specs=in_specs, out_specs=out_specs, check_vma=False)
```
